32 devices in a mesh: groups: 2 (over x), gx: 8 (over z, y), shot: 2 (over core).
Axes of the slice: x: 2, y: 2, z: 4, core: 2. Of those that a mesh axis runs over, the one named last changes fastest.
Arguments:
- src_now: float32 [8, 128, 64, 128], P(('groups', 'shot'), 'gx'), parts along dimension 0, may hold values from -6 to 6
- src_prev: float32 [8, 128, 64, 128], P(('groups', 'shot'), 'gx'), parts along dimension 0, may hold values from -6 to 6
- rec_now: float32 [8, 128, 64, 128], P(('groups', 'shot'), 'gx'), parts along dimension 0, may hold values from -6 to 6
- rec_prev: float32 [8, 128, 64, 128], P(('groups', 'shot'), 'gx'), parts along dimension 0, may hold values from -6 to 6
- courant_sq: float32 [256, 64, 128], P(('groups', 'gx')), parts along dimension 0, may hold values from 0.05 to 0.3
- wavelet: float32 [8, 4], P(('groups', 'shot')), parts along dimension 0, may hold values from -8 to 8
- traces: float32 [8, 4, 128], P(('groups', 'shot'), None, 'gx'), parts along dimension 0, may hold values from -6 to 6
- positions: int32 [8, 4], P(('groups', 'shot')), parts along dimension 0, may hold values from 0 to 127, as said below
Outputs:
- angle_image: float32 [16, 128, 32, 128], P(('groups', 'shot'), 'gx'), parts along dimension 0
The draws below stay inside these ranges and needn't reach their ends.
There are 2 independent parts, one for each index of `groups`. The reference program is written for one: setup_inputs(seed, part) draws one part's arguments, and reference() takes and returns one part's arrays. A program takes and returns all parts, laid end to end along the dimension named above; each array names one. Nothing has to cross between parts.
Inputs may be any that keep to these rules, and one draw needn't show every extreme that they name: `positions`: column 0 lies in 0 .. 127, columns 1 and 3 in 0 .. 127, column 2 in 0 .. 63; one shot of each patch has its source at x 128 - 1, y * 128 - 1, depth 64 - 1 and its receiver line at y 0.
All inputs are finite; a program needn't handle non-finite values.
Results may differ from the reference program's by a relative error of at most 0.0001.
Values sent between devices are 32-bit elements; how exact they have to be, the bound alone decides.
A program may use at most 192 MiB of HBM per device.

```python
import math
import jax
import jax.numpy as jnp
from jax import lax

NY = 128
NZ = 64
STEPS = 4
IMAGES = 2
LAGS = 49
ANGLES = 8
HALF = 24
NZH = 32
NX = 128
SHOTS = 4


def draw_positions(key, part):
    limits = jnp.array([NX, NY, NZ, NY], jnp.int32)
    raw = jax.random.randint(jax.random.fold_in(key, 7), (SHOTS, 4), 0, 1 << 20, dtype=jnp.int32)
    drawn = raw % limits[None, :]
    corner = jnp.array([NX - 1, NY - 1, NZ - 1, 0], jnp.int32)
    return drawn.at[0].set(corner)


def block_scale(rng, dims, cuts, least, top_value):
    gain = 1.0
    for axis_at, blocks in cuts:
        steps = jax.random.uniform(jax.random.fold_in(jax.random.fold_in(rng, 6), axis_at), (blocks,), jnp.float32, least / len(cuts), top_value / len(cuts))
        gain = gain * jnp.repeat(jnp.exp(steps), dims[axis_at] // blocks).reshape((-1,) + (1,) * (len(dims) - 1 - axis_at))
    return gain


def gaussian(key, shape, scale, reach, pieces=(), kind=jnp.bfloat16):
    entries = scale * jax.random.normal(key, shape, jnp.float32)
    if pieces:
        entries = entries * block_scale(key, shape, pieces, -0.22, 0.18)
    return jnp.clip(entries, -reach, reach).astype(kind)


def setup_inputs(seed: int = 0, part: int = 0) -> dict:
    seeds = jax.random.split(jax.random.key(seed), 9)
    part_keys = jax.random.split(jax.random.fold_in(seeds[8], part), 9)
    return {
        "src_now": gaussian(part_keys[0], (SHOTS, NX, NZ, NY), 1.0, 6.0, ((0, 2), (1, 8)), jnp.float32),
        "src_prev": gaussian(part_keys[1], (SHOTS, NX, NZ, NY), 1.0, 6.0, ((0, 2), (1, 8)), jnp.float32),
        "rec_now": gaussian(part_keys[2], (SHOTS, NX, NZ, NY), 1.0, 6.0, ((0, 2), (1, 8)), jnp.float32),
        "rec_prev": gaussian(part_keys[3], (SHOTS, NX, NZ, NY), 1.0, 6.0, ((0, 2), (1, 8)), jnp.float32),
        "courant_sq": jnp.clip(jnp.exp(math.log(0.3) - 1.7917595 * jax.random.uniform(part_keys[4], (NX, NZ, NY), jnp.float32) ** block_scale(part_keys[4], (NX, NZ, NY), ((0, 8),), -0.2, 0.2)), 0.05, 0.3),
        "wavelet": gaussian(part_keys[5], (SHOTS, STEPS), 2.0, 8.0, ((0, 2),), jnp.float32),
        "traces": gaussian(part_keys[6], (SHOTS, STEPS, NX), 1.0, 6.0, ((0, 2), (2, 8)), jnp.float32),
        "positions": draw_positions(jax.random.fold_in(jax.random.fold_in(seeds[8], part), 71), part),
    }


def laplace(field):
    padded = jnp.pad(field, ((0, 0), (1, 1), (1, 1), (1, 1)))
    beside = padded[:, 2:, 1:-1, 1:-1] + padded[:, :-2, 1:-1, 1:-1]
    beside = beside + padded[:, 1:-1, 2:, 1:-1] + padded[:, 1:-1, :-2, 1:-1]
    beside = beside + padded[:, 1:-1, 1:-1, 2:] + padded[:, 1:-1, 1:-1, :-2]
    return beside - 6.0 * field

def slant_stack(source, receiver):
    width = source.shape[1]
    spad = jnp.pad(source, ((0, 0), (HALF, HALF), (0, 0), (0, 0)))
    rpad = jnp.pad(receiver, ((0, 0), (HALF, HALF), (0, 0), (0, 0)))
    totals = [None] * ANGLES
    for index in range(LAGS):
        offset = index - HALF
        product = lax.optimization_barrier(jnp.sum(spad[:, HALF - offset:HALF - offset + width] * rpad[:, HALF + offset:HALF + offset + width], axis=0))
        for angle in range(ANGLES):
            moved = angle * abs(offset) // ANGLES
            piece = product[:, moved:moved + NZH, :]
            totals[angle] = piece if totals[angle] is None else totals[angle] + piece
    return jnp.stack(totals)

def reference(src_now, src_prev, rec_now, rec_prev, courant_sq, wavelet, traces, positions):
    ftype = src_now.dtype
    xgrid = jnp.arange(NX, dtype=jnp.int32)
    ygrid = jnp.arange(NY, dtype=jnp.int32)
    zgrid = jnp.arange(NZ, dtype=jnp.int32)
    source_mask = ((xgrid[None, :, None, None] == positions[:, 0, None, None, None]) & (zgrid[None, None, :, None] == positions[:, 2, None, None, None]) & (ygrid[None, None, None, :] == positions[:, 1, None, None, None])).astype(ftype)
    line_mask = (ygrid[None, :] == positions[:, 3, None]).astype(ftype)
    every = STEPS // IMAGES
    total = jnp.zeros((ANGLES, NX, NZH, NY), ftype)
    for step in range(STEPS):
        src_next = 2.0 * src_now - src_prev + courant_sq[None] * laplace(src_now) + wavelet[:, step, None, None, None] * source_mask
        rec_next = 2.0 * rec_now - rec_prev + courant_sq[None] * laplace(rec_now)
        rec_next = rec_next.at[:, :, 0, :].add(traces[:, STEPS - 1 - step, :, None] * line_mask[:, None, :])
        src_prev, src_now = (src_now, src_next)
        rec_prev, rec_now = (rec_now, rec_next)
        if (step + 1) % every == 0:
            total = total + slant_stack(src_now, rec_now)
    return total * (1.0 / math.sqrt(LAGS * SHOTS * IMAGES))
```

```python
import functools
import math

import jax
import jax.numpy as jnp
from jax import lax
from jax.experimental import pallas as pl
from jax.experimental.pallas import tpu as pltpu
from jax.sharding import PartitionSpec as P

STEPS = 4
IMAGES = 2
LAGS = 49
ANGLES = 8
HALF = (LAGS - 1) // 2
MESH = pl.DeviceIdType.MESH


def kernel(
    n,
    scale,
    rows,
    sent,
    positions,
    wavelet,
    traces,
    src_now,
    src_prev,
    rec_now,
    rec_prev,
    courant_hbm,
    out,
    level,
    courant,
    window,
    outgoing,
    image,
    from_core,
    summed,
    from_pair,
    product,
    load_sem,
    halo_send,
    halo_recv,
    pair_send,
    pair_recv,
    away_send,
    away_recv,
    near_send,
    near_recv,
    core_send,
    core_recv,
    out_send,
    out_recv,
):
    planes, depth, width = courant.shape
    block = planes // 2
    shots = src_now.shape[0]
    depth_out = out.shape[2]
    packs = from_core.shape[1]
    lanes = width // 2
    me = lax.axis_index("gx")
    core = lax.axis_index("shot")
    y = lax.rem(me, 2)
    pair = me + 1 - 2 * y
    other = 1 - core
    has_below = me >= 2
    has_above = me < n - 2
    has_away = ((y == 0) & has_above) | ((y == 1) & has_below)
    has_near = ((y == 0) & has_below) | ((y == 1) & has_above)
    parts = [
        ((block, block - 2), (2, block - 2), (planes - 2, 2), (0, 2)),
        ((1, block - 1), (block, block - 1), (planes - 1, 1), (0, 1)),
    ]

    loads = []
    for i, (ref, k, f) in enumerate(
        ((src_now, 1, 0), (rec_now, 1, 1), (src_prev, 0, 0), (rec_prev, 0, 1))
    ):
        loads.append(
            pltpu.make_async_copy(ref, level.at[k, f, :, pl.ds(1, planes)], load_sem.at[i])
        )
    loads.append(pltpu.make_async_copy(courant_hbm, courant, load_sem.at[4]))
    for load in loads:
        load.start()

    barrier = pltpu.get_barrier_semaphore()
    for step in (-2, -1, 1, 2):
        there = me + step

        @pl.when((there >= 0) & (there < n))
        def _():
            pl.semaphore_signal(barrier, inc=1, device_id={"gx": there}, device_id_type=MESH)

    pl.semaphore_signal(barrier, inc=1, device_id={"shot": other}, device_id_type=MESH)

    edge = jnp.zeros((rows, width), jnp.float32)
    full = jnp.zeros((depth, width), jnp.float32)

    @pl.when(me == 0)
    def _():
        for k in range(1, STEPS + 1):
            for f in range(2):
                for s in range(shots):
                    level[k, f, s, 0] = full

    @pl.when(me == n - 1)
    def _():
        for k in range(1, STEPS + 1):
            for f in range(2):
                for s in range(shots):
                    level[k, f, s, planes + 1] = full

    @pl.when(jnp.logical_not(has_below))
    def _():
        @pl.loop(0, HALF)
        def _(q):
            for g in range(IMAGES):
                for f in range(2):
                    window[g, f, q] = edge

    @pl.when(jnp.logical_not(has_above))
    def _():
        @pl.loop(0, HALF)
        def _(q):
            for g in range(IMAGES):
                for f in range(2):
                    window[g, f, HALF + 2 * planes + q] = edge

    peers = jnp.minimum(me, 2) + jnp.minimum(n - 1 - me, 2) + 1
    pl.semaphore_wait(barrier, peers)

    def halo(t, side):
        height = min(depth, rows + 1) if t == 0 else rows
        kept = pl.ds(0, height)
        source, target = (planes, 0) if side == 0 else (1, planes + 1)
        return pltpu.make_async_remote_copy(
            src_ref=level.at[1 + t, :, :, source, kept],
            dst_ref=level.at[1 + t, :, :, target, kept],
            send_sem=halo_send.at[t, side],
            recv_sem=halo_recv.at[t, side],
            device_id={"gx": me + 1 if side == 0 else me - 1},
            device_id_type=MESH,
        )

    def send_halo(t):
        @pl.when(me < n - 1)
        def _():
            halo(t, 0).start()

        @pl.when(me > 0)
        def _():
            halo(t, 1).start()

    def wait_halo(t):
        @pl.when(me > 0)
        def _():
            halo(t, 0).wait_recv()

        @pl.when(me < n - 1)
        def _():
            halo(t, 1).wait_recv()

    z_row = lax.broadcasted_iota(jnp.int32, (rows, width), 0)
    y_lane = lax.broadcasted_iota(jnp.int32, (rows, width), 1)
    first = me * planes

    def plane_step(t, x):
        speed = courant[x - 1, :rows]
        tall = depth if t == 0 else rows
        for s in range(shots):
            for f in range(2):
                now_tall = level[1 + t, f, s, x, :tall]
                now = now_tall[:rows]
                low = level[1 + t, f, s, x - 1, :rows]
                high = level[1 + t, f, s, x + 1, :rows]
                zeros = jnp.zeros((1, width), jnp.float32)
                deeper = jnp.concatenate([now_tall[1:], zeros], axis=0)[:rows]
                shallower = jnp.concatenate([zeros, now[: rows - 1]], axis=0)
                left = jnp.where(y_lane == 0, 0.0, pltpu.roll(now, 1, 1))
                right = jnp.where(y_lane == width - 1, 0.0, pltpu.roll(now, width - 1, 1))
                beside = low + high + deeper + shallower + left + right
                nxt = 2.0 * now - level[t, f, s, x, :rows] + speed * (beside - 6.0 * now)
                if f == 0:
                    amount = jnp.where(first + x - 1 == positions[s, 0], wavelet[s, t], 0.0)
                    hit = (z_row == positions[s, 2]) & (y_lane == positions[s, 1])
                else:
                    amount = traces[s, STEPS - 1 - t, x - 1]
                    hit = (z_row == 0) & (y_lane == positions[s, 3])
                level[2 + t, f, s, x, :rows] = nxt + jnp.where(hit, amount, 0.0)

    def steps(t, low, high):
        @pl.loop(low + 1, high + 1)
        def _(x):
            plane_step(t, x)

    def both_sides(t, low, high):
        count = high - low

        @pl.loop(0, 2 * count)
        def _(i):
            side = i // count
            x = low + i - side * count
            plane_step(t, 1 + x + side * (planes - 1 - 2 * x))

    def begin(g, i, yy):
        low, count = parts[g][i]
        return low + yy * (planes - 2 * low - count)

    def part_steps(t, g, i):
        at = begin(g, i, y)

        @pl.loop(0, parts[g][i][1])
        def _(j):
            plane_step(t, 1 + at + j)

    def pair_copy(g, i):
        at = begin(g, i, y)
        count = parts[g][i][1]
        return pltpu.make_async_remote_copy(
            src_ref=outgoing.at[g, :, pl.ds(at, count), pl.ds(0, sent)],
            dst_ref=window.at[g, :, pl.ds(HALF + planes * y + at, count), pl.ds(0, sent)],
            send_sem=pair_send.at[g, i],
            recv_sem=pair_recv.at[g, i],
            device_id={"gx": pair},
            device_id_type=MESH,
        )

    up_from, down_to = -block, HALF + 2 * planes

    def away_copy(g, i, relayed):
        yy = 1 - y if relayed else y
        at = planes * yy + begin(g, i, yy)
        count = parts[g][i][1]
        return pltpu.make_async_remote_copy(
            src_ref=window.at[g, :, pl.ds(HALF + at, count), pl.ds(0, sent)],
            dst_ref=window.at[
                g, :, pl.ds(at + up_from + y * (down_to - up_from), count), pl.ds(0, sent)
            ],
            send_sem=away_send.at[g, i, relayed],
            recv_sem=away_recv.at[g, i, relayed],
            device_id={"gx": me + 2 - 4 * y},
            device_id_type=MESH,
        )

    def near_copy(g, i, relayed):
        yy = 1 - y if relayed else y
        at = planes * yy + begin(g, i, yy)
        count = parts[g][i][1]
        return pltpu.make_async_remote_copy(
            src_ref=window.at[g, :, pl.ds(HALF + at, count), pl.ds(0, sent)],
            dst_ref=window.at[
                g, :, pl.ds(at + down_to + y * (up_from - down_to), count), pl.ds(0, sent)
            ],
            send_sem=near_send.at[g, i, relayed],
            recv_sem=near_recv.at[g, i, relayed],
            device_id={"gx": me - 2 + 4 * y},
            device_id_type=MESH,
        )

    def inner(g, i):
        return parts[g][i][0] >= block

    def start_away(g, i, relayed):
        if relayed or inner(g, i):
            @pl.when(has_away)
            def _():
                away_copy(g, i, relayed).start()

    def start_near(g, i, relayed):
        if not relayed or inner(g, i):
            @pl.when(has_near)
            def _():
                near_copy(g, i, relayed).start()

    first_half = y_lane < lanes

    def pack(g, i):
        at = begin(g, i, y)

        @pl.loop(0, parts[g][i][1])
        def _(j):
            x = at + j
            for f in range(2):
                one = level[2 * g + 3, f, 0, 1 + x, :rows]
                two = level[2 * g + 3, f, 1, 1 + x, :rows]
                halves = (
                    jnp.where(first_half, one, pltpu.roll(two, lanes, 1)),
                    jnp.where(first_half, pltpu.roll(one, lanes, 1), two),
                )
                window[g, f, HALF + planes * y + x] = jnp.where(y == 0, halves[0], halves[1])
                outgoing[g, f, x] = jnp.where(y == 0, halves[1], halves[0])

    def relay(g, i):
        pair_copy(g, i).wait_recv()
        start_away(g, i, 1)
        start_near(g, i, 1)

    def wait_far(g, block_at):
        if block_at < 0:
            relayed, low = (0, block) if block_at == -3 else (1, (block_at + 2) * -block + block)
            if block_at == -1:
                low = 0
        else:
            relayed, low = ((0, 0), (0, block), (1, block))[block_at - 4]
        for i, (start, count) in enumerate(parts[g]):
            if low <= start < low + block:
                @pl.when(has_near if block_at < 0 else has_away)
                def _():
                    (away_copy if block_at < 0 else near_copy)(g, i, relayed).wait_recv()

    def image_chunk(g, chunk, lags, fresh=False):
        @pl.loop(0, block)
        def _(x):
            at = HALF + chunk * block + x
            totals = [None] * ANGLES
            for h in lags:
                reach = depth_out + (ANGLES - 1) * h // ANGLES
                tall = min(rows, -(-reach // 8) * 8)
                value = window[g, 0, at - h, :tall] * window[g, 1, at + h, :tall]
                if h:
                    value = value + window[g, 0, at + h, :tall] * window[g, 1, at - h, :tall]
                if h > 1:
                    product[h % 4, :tall] = value
                for a in range(ANGLES):
                    moved = a * h // ANGLES
                    piece = product[h % 4, moved : moved + depth_out] if moved else value[:depth_out]
                    totals[a] = piece if totals[a] is None else totals[a] + piece
            for i in range(ANGLES // 2):
                even, odd = totals[2 * i], totals[2 * i + 1]
                low = first_half[:depth_out]
                folded = jnp.where(low, even, odd)
                folded = folded + pltpu.roll(jnp.where(low, odd, even), lanes, 1)
                if not fresh:
                    folded = folded + image[chunk, i, x]
                image[chunk, i, x] = folded

    def core_copy(chunk):
        return pltpu.make_async_remote_copy(
            src_ref=image.at[chunk, pl.ds(packs * other, packs)],
            dst_ref=from_core.at[chunk],
            send_sem=core_send.at[chunk],
            recv_sem=core_recv.at[chunk],
            device_id={"shot": other},
            device_id_type=MESH,
        )

    def out_copy(j):
        return pltpu.make_async_remote_copy(
            src_ref=summed.at[j],
            dst_ref=from_pair.at[j],
            send_sem=out_send.at[j],
            recv_sem=out_recv.at[j],
            device_id={"gx": pair},
            device_id_type=MESH,
        )

    def pass_on(chunk):
        j = chunk - 2 * (1 - y)
        core_copy(chunk).wait_recv()

        @pl.loop(0, block)
        def _(x):
            for i in range(packs):
                summed[j, i, x] = image[chunk, packs * core + i, x] + from_core[chunk, i, x]

        out_copy(j).start()

    def finish(j):
        chunk = 2 * y + j
        core_copy(chunk).wait_recv()
        out_copy(j).wait_recv()

        @pl.loop(0, block)
        def _(x):
            low = first_half[:depth_out]
            for i in range(packs):
                mine = image[chunk, packs * core + i, x] + from_core[chunk, i, x]
                theirs = from_pair[j, i, x]
                left = jnp.where(y == 0, mine, theirs) * scale
                right = jnp.where(y == 0, theirs, mine) * scale
                out[2 * i, j * block + x] = jnp.where(low, left, pltpu.roll(right, lanes, 1))
                out[2 * i + 1, j * block + x] = jnp.where(low, pltpu.roll(left, lanes, 1), right)

    loads[0].wait()
    loads[1].wait()
    send_halo(0)
    for load in loads[2:]:
        load.wait()
    steps(0, 1, planes - 1)
    part_steps(1, 0, 0)
    pack(0, 0)
    pair_copy(0, 0).start()
    start_away(0, 0, 0)
    start_near(0, 0, 0)
    part_steps(1, 0, 1)
    pack(0, 1)
    wait_halo(0)
    both_sides(0, 0, 1)
    send_halo(1)
    pair_copy(0, 1).start()
    start_near(0, 1, 0)
    steps(2, 3, planes - 3)
    steps(3, 4, planes - 4)
    relay(0, 0)
    wait_halo(1)
    both_sides(1, 0, 2)
    send_halo(2)
    for i in (2, 3):
        pack(0, i)
        pair_copy(0, i).start()
        start_away(0, i, 0)
        start_near(0, i, 0)
    both_sides(2, 1, 3)
    relay(0, 1)
    wait_halo(2)
    both_sides(2, 0, 1)
    send_halo(3)
    both_sides(3, 1, 4)
    for i in (0, 1):
        pack(1, i)
        pair_copy(1, i).start()
        start_away(1, i, 0)
        start_near(1, i, 0)
    relay(0, 2)
    relay(0, 3)
    near, far = range(block + 1), range(2 * block + 1, HALF + 1)
    middle, most = range(block + 1, 2 * block + 1), range(2 * block + 1)

    @pl.loop(1, 3)
    def _(chunk):
        image_chunk(0, chunk, near, True)

    wait_halo(3)
    both_sides(3, 0, 1)
    for i in (2, 3):
        pack(1, i)
        pair_copy(1, i).start()
        start_away(1, i, 0)
        start_near(1, i, 0)
    for at in (-3, -2, -1, 4, 5, 6):
        wait_far(0, at)

    @pl.loop(1, 3)
    def _(chunk):
        image_chunk(0, chunk, range(block + 1, HALF + 1))

    relay(1, 0)

    @pl.loop(0, 2)
    def _(i):
        image_chunk(0, 3 * i, range(HALF + 1), True)

    relay(1, 1)
    relay(1, 2)
    relay(1, 3)
    chunks = [c + y * (3 - 2 * c) for c in range(4)]
    wait_far(1, 4)
    wait_far(1, 5)
    wait_far(1, -1)
    image_chunk(1, chunks[2], range(HALF + 1))
    core_copy(chunks[2]).start()
    image_chunk(1, chunks[3], most)
    pass_on(chunks[2])
    image_chunk(1, chunks[1], most)
    image_chunk(1, chunks[0], near)
    wait_far(1, 6)
    image_chunk(1, chunks[3], far)
    core_copy(chunks[3]).start()
    wait_far(1, -2)
    wait_far(1, -3)
    image_chunk(1, chunks[1], far)
    core_copy(chunks[1]).start()
    pass_on(chunks[3])
    image_chunk(1, chunks[0], range(block + 1, HALF + 1))
    core_copy(chunks[0]).start()
    finish(1 - y)
    finish(y)

    for t in range(STEPS):
        @pl.when(me < n - 1)
        def _():
            halo(t, 0).wait_send()

        @pl.when(me > 0)
        def _():
            halo(t, 1).wait_send()

    for g in range(IMAGES):
        for i in range(len(parts[g])):
            pair_copy(g, i).wait_send()
            for relayed in range(2):
                if relayed or inner(g, i):
                    @pl.when(has_away)
                    def _():
                        away_copy(g, i, relayed).wait_send()
                if not relayed or inner(g, i):
                    @pl.when(has_near)
                    def _():
                        near_copy(g, i, relayed).wait_send()

    for chunk in range(4):
        core_copy(chunk).wait_send()
    for j in range(2):
        out_copy(j).wait_send()


def solution(mesh):
    n = mesh.shape["gx"]
    cores = mesh.shape["shot"]

    def local(src_now, src_prev, rec_now, rec_prev, courant_sq, wavelet, traces, positions):
        shots, planes, depth, width = src_now.shape
        depth_out = depth // 2
        reach = depth_out + (ANGLES - 1) * HALF // ANGLES
        rows = min(depth, -(-(reach + STEPS - 1) // 8) * 8)
        block = planes // 2
        assert n % 2 == 0 and cores == 2 and shots == 2 and 3 * block == HALF and width % 2 == 0
        angles_out = ANGLES // cores
        scale = 1.0 / math.sqrt(LAGS * shots * cores * IMAGES)
        vmem = pl.BlockSpec(memory_space=pltpu.VMEM)
        smem = pl.BlockSpec(memory_space=pltpu.SMEM)
        hbm = pl.BlockSpec(memory_space=pl.ANY)
        f32 = jnp.float32
        dma = pltpu.SemaphoreType.DMA
        return pl.pallas_call(
            functools.partial(kernel, n, scale, rows, reach),
            out_shape=jax.ShapeDtypeStruct((angles_out, planes, depth_out, width), f32),
            in_specs=[smem] * 3 + [hbm] * 5,
            out_specs=vmem,
            scratch_shapes=[
                pltpu.VMEM((STEPS + 2, 2, shots, planes + 2, depth, width), f32),
                pltpu.VMEM((planes, depth, width), f32),
                pltpu.VMEM((IMAGES, 2, 2 * planes + 2 * HALF, rows, width), f32),
                pltpu.VMEM((IMAGES, 2, planes, rows, width), f32),
                pltpu.VMEM((4, ANGLES // 2, block, depth_out, width), f32),
                pltpu.VMEM((4, angles_out // 2, block, depth_out, width), f32),
                pltpu.VMEM((2, angles_out // 2, block, depth_out, width), f32),
                pltpu.VMEM((2, angles_out // 2, block, depth_out, width), f32),
                pltpu.VMEM((4, rows, width), f32),
                dma((5,)),
                dma((STEPS, 2)),
                dma((STEPS, 2)),
                dma((IMAGES, 4)),
                dma((IMAGES, 4)),
                dma((IMAGES, 4, 2)),
                dma((IMAGES, 4, 2)),
                dma((IMAGES, 4, 2)),
                dma((IMAGES, 4, 2)),
                dma((4,)),
                dma((4,)),
                dma((2,)),
                dma((2,)),
            ],
            compiler_params=pltpu.CompilerParams(
                collective_id=0, has_side_effects=True, vmem_limit_bytes=60 * 1024 * 1024
            ),
        )(positions, wavelet, traces, src_now, src_prev, rec_now, rec_prev, courant_sq)

    placed = (
        P(("groups", "shot"), "gx", None, None),
        P(("groups", "shot"), "gx", None, None),
        P(("groups", "shot"), "gx", None, None),
        P(("groups", "shot"), "gx", None, None),
        P(("groups", "gx"), None, None),
        P(("groups", "shot"), None),
        P(("groups", "shot"), None, "gx"),
        P(("groups", "shot"), None),
    )
    return jax.shard_map(
        local,
        mesh=mesh,
        in_specs=placed,
        out_specs=P(("groups", "shot"), "gx", None, None),
        check_vma=False,
    )
```

```python
import functools
import math

import jax
import jax.numpy as jnp
from jax import lax
from jax.experimental import pallas as pl
from jax.experimental.pallas import tpu as pltpu
from jax.sharding import PartitionSpec as P

STEPS = 4
IMAGES = 2
LAGS = 49
ANGLES = 8
HALF = (LAGS - 1) // 2
MESH = pl.DeviceIdType.MESH


def kernel(
    n,
    scale,
    rows,
    sent,
    positions,
    wavelet,
    traces,
    src_now,
    src_prev,
    rec_now,
    rec_prev,
    courant_hbm,
    out,
    level,
    courant,
    window,
    outgoing,
    image,
    from_core,
    summed,
    from_pair,
    product,
    load_sem,
    halo_send,
    halo_recv,
    pair_send,
    pair_recv,
    away_send,
    away_recv,
    near_send,
    near_recv,
    core_send,
    core_recv,
    out_send,
    out_recv,
):
    planes, depth, width = courant.shape
    block = planes // 2
    shots = src_now.shape[0]
    depth_out = out.shape[2]
    packs = from_core.shape[1]
    lanes = width // 2
    me = lax.axis_index("gx")
    core = lax.axis_index("shot")
    y = lax.rem(me, 2)
    pair = me + 1 - 2 * y
    other = 1 - core
    has_below = me >= 2
    has_above = me < n - 2
    has_away = ((y == 0) & has_above) | ((y == 1) & has_below)
    has_near = ((y == 0) & has_below) | ((y == 1) & has_above)
    parts = [
        ((block, block - 2), (2, block - 2), (planes - 2, 2), (0, 2)),
        ((block, 2), (block + 2, 2), (4, block - 4), (0, 4), (planes - 4, 4)),
    ]

    loads = []
    for i, (ref, k, f) in enumerate(
        ((src_now, 1, 0), (rec_now, 1, 1), (src_prev, 0, 0), (rec_prev, 0, 1))
    ):
        loads.append(
            pltpu.make_async_copy(ref, level.at[k, f, :, pl.ds(1, planes)], load_sem.at[i])
        )
    loads.append(pltpu.make_async_copy(courant_hbm, courant, load_sem.at[4]))
    for load in loads:
        load.start()

    barrier = pltpu.get_barrier_semaphore()
    for step in (-2, -1, 1, 2):
        there = me + step

        @pl.when((there >= 0) & (there < n))
        def _():
            pl.semaphore_signal(barrier, inc=1, device_id={"gx": there}, device_id_type=MESH)

    pl.semaphore_signal(barrier, inc=1, device_id={"shot": other}, device_id_type=MESH)

    edge = jnp.zeros((rows, width), jnp.float32)
    full = jnp.zeros((depth, width), jnp.float32)

    @pl.when(me == 0)
    def _():
        for k in range(1, STEPS + 1):
            for f in range(2):
                for s in range(shots):
                    level[k, f, s, 0] = full

    @pl.when(me == n - 1)
    def _():
        for k in range(1, STEPS + 1):
            for f in range(2):
                for s in range(shots):
                    level[k, f, s, planes + 1] = full

    @pl.when(jnp.logical_not(has_below))
    def _():
        @pl.loop(0, HALF)
        def _(q):
            for g in range(IMAGES):
                for f in range(2):
                    window[g, f, q] = edge

    @pl.when(jnp.logical_not(has_above))
    def _():
        @pl.loop(0, HALF)
        def _(q):
            for g in range(IMAGES):
                for f in range(2):
                    window[g, f, HALF + 2 * planes + q] = edge

    peers = jnp.minimum(me, 2) + jnp.minimum(n - 1 - me, 2) + 1
    pl.semaphore_wait(barrier, peers)

    def halo(t, side):
        height = min(depth, rows + 1) if t == 0 else rows
        kept = pl.ds(0, height)
        source, target = (planes, 0) if side == 0 else (1, planes + 1)
        return pltpu.make_async_remote_copy(
            src_ref=level.at[1 + t, :, :, source, kept],
            dst_ref=level.at[1 + t, :, :, target, kept],
            send_sem=halo_send.at[t, side],
            recv_sem=halo_recv.at[t, side],
            device_id={"gx": me + 1 if side == 0 else me - 1},
            device_id_type=MESH,
        )

    def send_halo(t):
        @pl.when(me < n - 1)
        def _():
            halo(t, 0).start()

        @pl.when(me > 0)
        def _():
            halo(t, 1).start()

    def wait_halo(t):
        @pl.when(me > 0)
        def _():
            halo(t, 0).wait_recv()

        @pl.when(me < n - 1)
        def _():
            halo(t, 1).wait_recv()

    z_row = lax.broadcasted_iota(jnp.int32, (rows, width), 0)
    y_lane = lax.broadcasted_iota(jnp.int32, (rows, width), 1)
    first = me * planes

    def plane_step(t, x):
        speed = courant[x - 1, :rows]
        tall = depth if t == 0 else rows
        for s in range(shots):
            for f in range(2):
                now_tall = level[1 + t, f, s, x, :tall]
                now = now_tall[:rows]
                low = level[1 + t, f, s, x - 1, :rows]
                high = level[1 + t, f, s, x + 1, :rows]
                zeros = jnp.zeros((1, width), jnp.float32)
                deeper = jnp.concatenate([now_tall[1:], zeros], axis=0)[:rows]
                shallower = jnp.concatenate([zeros, now[: rows - 1]], axis=0)
                left = jnp.where(y_lane == 0, 0.0, pltpu.roll(now, 1, 1))
                right = jnp.where(y_lane == width - 1, 0.0, pltpu.roll(now, width - 1, 1))
                beside = low + high + deeper + shallower + left + right
                nxt = 2.0 * now - level[t, f, s, x, :rows] + speed * (beside - 6.0 * now)
                if f == 0:
                    amount = jnp.where(first + x - 1 == positions[s, 0], wavelet[s, t], 0.0)
                    hit = (z_row == positions[s, 2]) & (y_lane == positions[s, 1])
                else:
                    amount = traces[s, STEPS - 1 - t, x - 1]
                    hit = (z_row == 0) & (y_lane == positions[s, 3])
                level[2 + t, f, s, x, :rows] = nxt + jnp.where(hit, amount, 0.0)

    def steps(t, low, high):
        @pl.loop(low + 1, high + 1)
        def _(x):
            plane_step(t, x)

    def both_sides(t, low, high):
        count = high - low

        @pl.loop(0, 2 * count)
        def _(i):
            side = i // count
            x = low + i - side * count
            plane_step(t, 1 + x + side * (planes - 1 - 2 * x))

    def begin(g, i, yy):
        low, count = parts[g][i]
        return low + yy * (planes - 2 * low - count)

    def part_steps(t, g, i):
        at = begin(g, i, y)

        @pl.loop(0, parts[g][i][1])
        def _(j):
            plane_step(t, 1 + at + j)

    def pair_copy(g, i):
        at = begin(g, i, y)
        count = parts[g][i][1]
        return pltpu.make_async_remote_copy(
            src_ref=outgoing.at[g, :, pl.ds(at, count), pl.ds(0, sent)],
            dst_ref=window.at[g, :, pl.ds(HALF + planes * y + at, count), pl.ds(0, sent)],
            send_sem=pair_send.at[g, i],
            recv_sem=pair_recv.at[g, i],
            device_id={"gx": pair},
            device_id_type=MESH,
        )

    up_from, down_to = -block, HALF + 2 * planes

    def away_copy(g, i, relayed):
        yy = 1 - y if relayed else y
        at = planes * yy + begin(g, i, yy)
        count = parts[g][i][1]
        return pltpu.make_async_remote_copy(
            src_ref=window.at[g, :, pl.ds(HALF + at, count), pl.ds(0, sent)],
            dst_ref=window.at[
                g, :, pl.ds(at + up_from + y * (down_to - up_from), count), pl.ds(0, sent)
            ],
            send_sem=away_send.at[g, i, relayed],
            recv_sem=away_recv.at[g, i, relayed],
            device_id={"gx": me + 2 - 4 * y},
            device_id_type=MESH,
        )

    def near_copy(g, i, relayed):
        yy = 1 - y if relayed else y
        at = planes * yy + begin(g, i, yy)
        count = parts[g][i][1]
        return pltpu.make_async_remote_copy(
            src_ref=window.at[g, :, pl.ds(HALF + at, count), pl.ds(0, sent)],
            dst_ref=window.at[
                g, :, pl.ds(at + down_to + y * (up_from - down_to), count), pl.ds(0, sent)
            ],
            send_sem=near_send.at[g, i, relayed],
            recv_sem=near_recv.at[g, i, relayed],
            device_id={"gx": me - 2 + 4 * y},
            device_id_type=MESH,
        )

    def inner(g, i):
        return parts[g][i][0] >= block

    def start_away(g, i, relayed):
        if relayed or inner(g, i):
            @pl.when(has_away)
            def _():
                away_copy(g, i, relayed).start()

    def start_near(g, i, relayed):
        if not relayed or inner(g, i):
            @pl.when(has_near)
            def _():
                near_copy(g, i, relayed).start()

    first_half = y_lane < lanes

    def pack(g, i):
        at = begin(g, i, y)

        @pl.loop(0, parts[g][i][1])
        def _(j):
            x = at + j
            for f in range(2):
                one = level[2 * g + 3, f, 0, 1 + x, :rows]
                two = level[2 * g + 3, f, 1, 1 + x, :rows]
                halves = (
                    jnp.where(first_half, one, pltpu.roll(two, lanes, 1)),
                    jnp.where(first_half, pltpu.roll(one, lanes, 1), two),
                )
                window[g, f, HALF + planes * y + x] = jnp.where(y == 0, halves[0], halves[1])
                outgoing[g, f, x] = jnp.where(y == 0, halves[1], halves[0])

    def relay(g, i):
        pair_copy(g, i).wait_recv()
        start_away(g, i, 1)
        start_near(g, i, 1)

    def wait_far(g, block_at):
        if block_at < 0:
            relayed, low = ((1, 0), (1, block), (0, block))[-1 - block_at]
        else:
            relayed, low = ((0, 0), (0, block), (1, block))[block_at - 4]
        for i, (start, count) in enumerate(parts[g]):
            if low <= start < low + block:
                @pl.when(has_near if block_at < 0 else has_away)
                def _():
                    (away_copy if block_at < 0 else near_copy)(g, i, relayed).wait_recv()

    def image_chunk(g, chunk, lags, fresh=False):
        @pl.loop(0, block)
        def _(x):
            at = HALF + chunk * block + x
            totals = [None] * ANGLES
            for h in lags:
                reach = depth_out + (ANGLES - 1) * h // ANGLES
                tall = min(rows, -(-reach // 8) * 8)
                value = window[g, 0, at - h, :tall] * window[g, 1, at + h, :tall]
                if h:
                    value = value + window[g, 0, at + h, :tall] * window[g, 1, at - h, :tall]
                if h > 1:
                    product[h % 4, :tall] = value
                for a in range(ANGLES):
                    moved = a * h // ANGLES
                    piece = product[h % 4, moved : moved + depth_out] if moved else value[:depth_out]
                    totals[a] = piece if totals[a] is None else totals[a] + piece
            for i in range(ANGLES // 2):
                even, odd = totals[2 * i], totals[2 * i + 1]
                low = first_half[:depth_out]
                folded = jnp.where(low, even, odd)
                folded = folded + pltpu.roll(jnp.where(low, odd, even), lanes, 1)
                if not fresh:
                    folded = folded + image[chunk, i, x]
                image[chunk, i, x] = folded

    def core_copy(chunk):
        return pltpu.make_async_remote_copy(
            src_ref=image.at[chunk, pl.ds(packs * other, packs)],
            dst_ref=from_core.at[chunk],
            send_sem=core_send.at[chunk],
            recv_sem=core_recv.at[chunk],
            device_id={"shot": other},
            device_id_type=MESH,
        )

    def out_copy(j):
        return pltpu.make_async_remote_copy(
            src_ref=summed.at[j],
            dst_ref=from_pair.at[j],
            send_sem=out_send.at[j],
            recv_sem=out_recv.at[j],
            device_id={"gx": pair},
            device_id_type=MESH,
        )

    def pass_on(chunk):
        j = chunk - 2 * (1 - y)
        core_copy(chunk).wait_recv()

        @pl.loop(0, block)
        def _(x):
            for i in range(packs):
                summed[j, i, x] = image[chunk, packs * core + i, x] + from_core[chunk, i, x]

        out_copy(j).start()

    def finish(j):
        chunk = 2 * y + j
        core_copy(chunk).wait_recv()
        out_copy(j).wait_recv()

        @pl.loop(0, block)
        def _(x):
            low = first_half[:depth_out]
            for i in range(packs):
                mine = image[chunk, packs * core + i, x] + from_core[chunk, i, x]
                theirs = from_pair[j, i, x]
                left = jnp.where(y == 0, mine, theirs) * scale
                right = jnp.where(y == 0, theirs, mine) * scale
                out[2 * i, j * block + x] = jnp.where(low, left, pltpu.roll(right, lanes, 1))
                out[2 * i + 1, j * block + x] = jnp.where(low, pltpu.roll(left, lanes, 1), right)

    loads[0].wait()
    loads[1].wait()
    send_halo(0)
    for load in loads[2:]:
        load.wait()
    steps(0, 1, planes - 1)
    part_steps(1, 0, 0)
    pack(0, 0)
    pair_copy(0, 0).start()
    start_away(0, 0, 0)
    start_near(0, 0, 0)
    part_steps(1, 0, 1)
    pack(0, 1)
    wait_halo(0)
    both_sides(0, 0, 1)
    send_halo(1)
    pair_copy(0, 1).start()
    start_near(0, 1, 0)
    steps(2, 3, planes - 3)
    steps(3, 4, planes - 4)
    for i in range(3):
        pack(1, i)
    start_away(1, 0, 0)
    relay(0, 0)
    wait_halo(1)
    both_sides(1, 0, 2)
    send_halo(2)
    for i in (2, 3):
        pack(0, i)
        pair_copy(0, i).start()
        start_away(0, i, 0)
        start_near(0, i, 0)
    start_away(1, 1, 0)
    both_sides(2, 1, 3)
    relay(0, 1)
    wait_halo(2)
    both_sides(2, 0, 1)
    send_halo(3)
    for i in (2, 0, 1):
        pair_copy(1, i).start()
    both_sides(3, 1, 4)
    relay(0, 2)
    relay(0, 3)
    for i in (2, 0, 1):
        start_near(1, i, 0)
    near, far = range(block + 1), range(2 * block + 1, HALF + 1)
    rest, most = range(block + 1, HALF + 1), range(2 * block + 1)

    @pl.loop(1, 3)
    def _(chunk):
        image_chunk(0, chunk, near, True)

    wait_halo(3)
    both_sides(3, 0, 1)
    for i in (3, 4):
        pack(1, i)
        pair_copy(1, i).start()
        start_away(1, i, 0)
        start_near(1, i, 0)
    for at in (-3, -2, -1, 4, 5, 6):
        wait_far(0, at)
    image_chunk(0, 1, rest)
    relay(1, 2)
    image_chunk(0, 2, rest)
    for i in range(2):
        pair_copy(1, i).wait_recv()
        start_away(1, i, 1)
    image_chunk(0, 0, range(HALF + 1), True)
    relay(1, 3)
    image_chunk(0, 3, range(HALF + 1), True)
    relay(1, 4)
    for i in (1, 0):
        start_near(1, i, 1)
    chunks = [c + y * (3 - 2 * c) for c in range(4)]
    wait_far(1, 4)
    wait_far(1, 5)
    wait_far(1, -1)
    image_chunk(1, chunks[2], range(HALF + 1))
    core_copy(chunks[2]).start()
    image_chunk(1, chunks[3], most)
    pass_on(chunks[2])
    image_chunk(1, chunks[1], most)
    image_chunk(1, chunks[0], near)
    wait_far(1, 6)
    image_chunk(1, chunks[3], far)
    core_copy(chunks[3]).start()
    wait_far(1, -2)
    wait_far(1, -3)
    image_chunk(1, chunks[1], far)
    core_copy(chunks[1]).start()
    pass_on(chunks[3])
    image_chunk(1, chunks[0], rest)
    core_copy(chunks[0]).start()
    finish(1 - y)
    finish(y)

    for t in range(STEPS):
        @pl.when(me < n - 1)
        def _():
            halo(t, 0).wait_send()

        @pl.when(me > 0)
        def _():
            halo(t, 1).wait_send()

    for g in range(IMAGES):
        for i in range(len(parts[g])):
            pair_copy(g, i).wait_send()
            for relayed in range(2):
                if relayed or inner(g, i):
                    @pl.when(has_away)
                    def _():
                        away_copy(g, i, relayed).wait_send()
                if not relayed or inner(g, i):
                    @pl.when(has_near)
                    def _():
                        near_copy(g, i, relayed).wait_send()

    for chunk in range(4):
        core_copy(chunk).wait_send()
    for j in range(2):
        out_copy(j).wait_send()


def solution(mesh):
    n = mesh.shape["gx"]
    cores = mesh.shape["shot"]

    def local(src_now, src_prev, rec_now, rec_prev, courant_sq, wavelet, traces, positions):
        shots, planes, depth, width = src_now.shape
        depth_out = depth // 2
        reach = depth_out + (ANGLES - 1) * HALF // ANGLES
        rows = min(depth, -(-(reach + STEPS - 1) // 8) * 8)
        block = planes // 2
        assert n % 2 == 0 and cores == 2 and shots == 2 and 3 * block == HALF and width % 2 == 0
        angles_out = ANGLES // cores
        scale = 1.0 / math.sqrt(LAGS * shots * cores * IMAGES)
        vmem = pl.BlockSpec(memory_space=pltpu.VMEM)
        smem = pl.BlockSpec(memory_space=pltpu.SMEM)
        hbm = pl.BlockSpec(memory_space=pl.ANY)
        f32 = jnp.float32
        dma = pltpu.SemaphoreType.DMA
        return pl.pallas_call(
            functools.partial(kernel, n, scale, rows, reach),
            out_shape=jax.ShapeDtypeStruct((angles_out, planes, depth_out, width), f32),
            in_specs=[smem] * 3 + [hbm] * 5,
            out_specs=vmem,
            scratch_shapes=[
                pltpu.VMEM((STEPS + 2, 2, shots, planes + 2, depth, width), f32),
                pltpu.VMEM((planes, depth, width), f32),
                pltpu.VMEM((IMAGES, 2, 2 * planes + 2 * HALF, rows, width), f32),
                pltpu.VMEM((IMAGES, 2, planes, rows, width), f32),
                pltpu.VMEM((4, ANGLES // 2, block, depth_out, width), f32),
                pltpu.VMEM((4, angles_out // 2, block, depth_out, width), f32),
                pltpu.VMEM((2, angles_out // 2, block, depth_out, width), f32),
                pltpu.VMEM((2, angles_out // 2, block, depth_out, width), f32),
                pltpu.VMEM((4, rows, width), f32),
                dma((5,)),
                dma((STEPS, 2)),
                dma((STEPS, 2)),
                dma((IMAGES, 5)),
                dma((IMAGES, 5)),
                dma((IMAGES, 5, 2)),
                dma((IMAGES, 5, 2)),
                dma((IMAGES, 5, 2)),
                dma((IMAGES, 5, 2)),
                dma((4,)),
                dma((4,)),
                dma((2,)),
                dma((2,)),
            ],
            compiler_params=pltpu.CompilerParams(
                collective_id=0, has_side_effects=True, vmem_limit_bytes=60 * 1024 * 1024
            ),
        )(positions, wavelet, traces, src_now, src_prev, rec_now, rec_prev, courant_sq)

    placed = (
        P(("groups", "shot"), "gx", None, None),
        P(("groups", "shot"), "gx", None, None),
        P(("groups", "shot"), "gx", None, None),
        P(("groups", "shot"), "gx", None, None),
        P(("groups", "gx"), None, None),
        P(("groups", "shot"), None),
        P(("groups", "shot"), None, "gx"),
        P(("groups", "shot"), None),
    )
    return jax.shard_map(
        local,
        mesh=mesh,
        in_specs=placed,
        out_specs=P(("groups", "shot"), "gx", None, None),
        check_vma=False,
    )
```

```python
import functools
import math

import jax
import jax.numpy as jnp
from jax import lax
from jax.experimental import pallas as pl
from jax.experimental.pallas import tpu as pltpu
from jax.sharding import PartitionSpec as P

STEPS = 4
IMAGES = 2
LAGS = 49
ANGLES = 8
HALF = (LAGS - 1) // 2
MESH = pl.DeviceIdType.MESH


def kernel(
    n,
    scale,
    rows,
    sent,
    positions,
    wavelet,
    traces,
    src_now,
    src_prev,
    rec_now,
    rec_prev,
    courant_hbm,
    out,
    level,
    courant,
    window,
    outgoing,
    image,
    from_core,
    summed,
    from_pair,
    product,
    passing,
    result,
    load_sem,
    store_sem,
    halo_send,
    halo_recv,
    pair_send,
    pair_recv,
    away_send,
    away_recv,
    near_send,
    near_recv,
    pass_send,
    pass_recv,
    core_send,
    core_recv,
    out_send,
    out_recv,
):
    planes, depth, width = courant.shape
    block = planes // 2
    shots = src_now.shape[0]
    depth_out = out.shape[2]
    packs = from_core.shape[1]
    lanes = width // 2
    me = lax.axis_index("gx")
    core = lax.axis_index("shot")
    y = lax.rem(me, 2)
    pair = me + 1 - 2 * y
    other = 1 - core
    has_below = me >= 2
    has_above = me < n - 2
    has_away = ((y == 0) & has_above) | ((y == 1) & has_below)
    has_near = ((y == 0) & has_below) | ((y == 1) & has_above)
    by_pair = ()
    parts = [
        ((block, block - 2), (2, block - 2), (planes - 2, 2), (0, 2)),
        ((block, 2), (block + 2, 2), (4, block - 4), (0, 4), (planes - 4, 4)),
    ]

    loads = []
    for i, (ref, k, f) in enumerate(
        ((src_now, 1, 0), (rec_now, 1, 1), (src_prev, 0, 0), (rec_prev, 0, 1))
    ):
        loads.append(
            pltpu.make_async_copy(ref, level.at[k, f, :, pl.ds(1, planes)], load_sem.at[i])
        )
    loads.append(pltpu.make_async_copy(courant_hbm, courant, load_sem.at[4]))
    for load in loads:
        load.start()

    barrier = pltpu.get_barrier_semaphore()
    for step in (-2, -1, 1, 2):
        there = me + step

        @pl.when((there >= 0) & (there < n))
        def _():
            pl.semaphore_signal(barrier, inc=1, device_id={"gx": there}, device_id_type=MESH)

    pl.semaphore_signal(barrier, inc=1, device_id={"shot": other}, device_id_type=MESH)

    edge = jnp.zeros((rows, width), jnp.float32)
    full = jnp.zeros((depth, width), jnp.float32)

    @pl.when(me == 0)
    def _():
        for k in range(1, STEPS + 1):
            for f in range(2):
                for s in range(shots):
                    level[k, f, s, 0] = full

    @pl.when(me == n - 1)
    def _():
        for k in range(1, STEPS + 1):
            for f in range(2):
                for s in range(shots):
                    level[k, f, s, planes + 1] = full

    @pl.when(jnp.logical_not(has_below))
    def _():
        @pl.loop(0, HALF)
        def _(q):
            for g in range(IMAGES):
                for f in range(2):
                    window[g, f, q] = edge

    @pl.when(jnp.logical_not(has_above))
    def _():
        @pl.loop(0, HALF)
        def _(q):
            for g in range(IMAGES):
                for f in range(2):
                    window[g, f, HALF + 2 * planes + q] = edge

    peers = jnp.minimum(me, 2) + jnp.minimum(n - 1 - me, 2) + 1
    pl.semaphore_wait(barrier, peers)

    def halo(t, side):
        height = min(depth, sent + STEPS - 1 - t)
        kept = pl.ds(0, height)
        source, target = (planes, 0) if side == 0 else (1, planes + 1)
        return pltpu.make_async_remote_copy(
            src_ref=level.at[1 + t, :, :, source, kept],
            dst_ref=level.at[1 + t, :, :, target, kept],
            send_sem=halo_send.at[t, side],
            recv_sem=halo_recv.at[t, side],
            device_id={"gx": me + 1 if side == 0 else me - 1},
            device_id_type=MESH,
        )

    def passing_copy(t):
        kept = pl.ds(0, min(depth, sent + STEPS - 1 - t))
        return pltpu.make_async_remote_copy(
            src_ref=level.at[1 + t, :, :, 1 + y * (planes - 1), kept],
            dst_ref=passing.at[t % 2, :, :, kept],
            send_sem=pass_send.at[t % 2, 0],
            recv_sem=pass_recv.at[t % 2, 0],
            device_id={"gx": pair},
            device_id_type=MESH,
        )

    def passed_copy(t):
        kept = pl.ds(0, min(depth, sent + STEPS - 1 - t))
        return pltpu.make_async_remote_copy(
            src_ref=passing.at[t % 2, :, :, kept],
            dst_ref=level.at[1 + t, :, :, y * (planes + 1), kept],
            send_sem=pass_send.at[t % 2, 1],
            recv_sem=pass_recv.at[t % 2, 1],
            device_id={"gx": me + 2 - 4 * y},
            device_id_type=MESH,
        )

    def each_halo(t, act_side, act_pass):
        for side in range(2):
            @pl.when(y == side)
            def _(side=side):
                act_side(halo(t, side))

            if t not in by_pair:
                @pl.when((y != side) & ((me < n - 1) if side == 0 else (me > 0)))
                def _(side=side):
                    act_side(halo(t, side))

        if t in by_pair:
            @pl.when(has_near)
            def _():
                act_pass(passing_copy(t))

    def send_halo(t):
        each_halo(t, lambda c: c.start(), lambda c: c.start())

    def pass_halo(t):
        @pl.when(has_away)
        def _():
            passing_copy(t).wait_recv()
            passed_copy(t).start()

    def wait_halo(t):
        for side in range(2):
            @pl.when(y != side)
            def _(side=side):
                halo(t, side).wait_recv()

            if t not in by_pair:
                @pl.when((y == side) & ((me > 0) if side == 0 else (me < n - 1)))
                def _(side=side):
                    halo(t, side).wait_recv()

        if t in by_pair:
            @pl.when(has_near)
            def _():
                passed_copy(t).wait_recv()

    z_row = lax.broadcasted_iota(jnp.int32, (rows, width), 0)
    y_lane = lax.broadcasted_iota(jnp.int32, (rows, width), 1)
    first = me * planes

    def plane_step(t, x):
        speed = courant[x - 1, :rows]
        tall = depth if t == 0 else rows
        for s in range(shots):
            for f in range(2):
                now_tall = level[1 + t, f, s, x, :tall]
                now = now_tall[:rows]
                low = level[1 + t, f, s, x - 1, :rows]
                high = level[1 + t, f, s, x + 1, :rows]
                zeros = jnp.zeros((1, width), jnp.float32)
                deeper = jnp.concatenate([now_tall[1:], zeros], axis=0)[:rows]
                shallower = jnp.concatenate([zeros, now[: rows - 1]], axis=0)
                left = jnp.where(y_lane == 0, 0.0, pltpu.roll(now, 1, 1))
                right = jnp.where(y_lane == width - 1, 0.0, pltpu.roll(now, width - 1, 1))
                beside = low + high + deeper + shallower + left + right
                nxt = 2.0 * now - level[t, f, s, x, :rows] + speed * (beside - 6.0 * now)
                if f == 0:
                    amount = jnp.where(first + x - 1 == positions[s, 0], wavelet[s, t], 0.0)
                    hit = (z_row == positions[s, 2]) & (y_lane == positions[s, 1])
                else:
                    amount = traces[s, STEPS - 1 - t, x - 1]
                    hit = (z_row == 0) & (y_lane == positions[s, 3])
                level[2 + t, f, s, x, :rows] = nxt + jnp.where(hit, amount, 0.0)

    def steps(t, low, high):
        @pl.loop(low + 1, high + 1)
        def _(x):
            plane_step(t, x)

    def both_sides(t, low, high):
        count = high - low

        @pl.loop(0, 2 * count)
        def _(i):
            side = i // count
            x = low + i - side * count
            plane_step(t, 1 + x + side * (planes - 1 - 2 * x))

    def begin(g, i, yy):
        low, count = parts[g][i]
        return low + yy * (planes - 2 * low - count)

    def mirror_steps(t, low, count):
        at = low + y * (planes - 2 * low - count)

        @pl.loop(0, count)
        def _(j):
            plane_step(t, 1 + at + j)

    def part_steps(t, g, i):
        at = begin(g, i, y)

        @pl.loop(0, parts[g][i][1])
        def _(j):
            plane_step(t, 1 + at + j)

    def pair_copy(g, i):
        at = begin(g, i, y)
        count = parts[g][i][1]
        return pltpu.make_async_remote_copy(
            src_ref=outgoing.at[g, :, pl.ds(at, count), pl.ds(0, sent)],
            dst_ref=window.at[g, :, pl.ds(HALF + planes * y + at, count), pl.ds(0, sent)],
            send_sem=pair_send.at[g, i],
            recv_sem=pair_recv.at[g, i],
            device_id={"gx": pair},
            device_id_type=MESH,
        )

    up_from, down_to = -block, HALF + 2 * planes

    def away_copy(g, i, relayed):
        yy = 1 - y if relayed else y
        at = planes * yy + begin(g, i, yy)
        count = parts[g][i][1]
        return pltpu.make_async_remote_copy(
            src_ref=window.at[g, :, pl.ds(HALF + at, count), pl.ds(0, sent)],
            dst_ref=window.at[
                g, :, pl.ds(at + up_from + y * (down_to - up_from), count), pl.ds(0, sent)
            ],
            send_sem=away_send.at[g, i, relayed],
            recv_sem=away_recv.at[g, i, relayed],
            device_id={"gx": me + 2 - 4 * y},
            device_id_type=MESH,
        )

    def near_copy(g, i, relayed):
        yy = 1 - y if relayed else y
        at = planes * yy + begin(g, i, yy)
        count = parts[g][i][1]
        return pltpu.make_async_remote_copy(
            src_ref=window.at[g, :, pl.ds(HALF + at, count), pl.ds(0, sent)],
            dst_ref=window.at[
                g, :, pl.ds(at + down_to + y * (up_from - down_to), count), pl.ds(0, sent)
            ],
            send_sem=near_send.at[g, i, relayed],
            recv_sem=near_recv.at[g, i, relayed],
            device_id={"gx": me - 2 + 4 * y},
            device_id_type=MESH,
        )

    def inner(g, i):
        return parts[g][i][0] >= block

    def start_away(g, i, relayed):
        if relayed or inner(g, i):
            @pl.when(has_away)
            def _():
                away_copy(g, i, relayed).start()

    def start_near(g, i, relayed):
        if not relayed or inner(g, i):
            @pl.when(has_near)
            def _():
                near_copy(g, i, relayed).start()

    first_half = y_lane < lanes

    def pack(g, i):
        at = begin(g, i, y)

        @pl.loop(0, parts[g][i][1])
        def _(j):
            x = at + j
            for f in range(2):
                one = level[2 * g + 3, f, 0, 1 + x, :rows]
                two = level[2 * g + 3, f, 1, 1 + x, :rows]
                halves = (
                    jnp.where(first_half, one, pltpu.roll(two, lanes, 1)),
                    jnp.where(first_half, pltpu.roll(one, lanes, 1), two),
                )
                window[g, f, HALF + planes * y + x] = jnp.where(y == 0, halves[0], halves[1])
                outgoing[g, f, x] = jnp.where(y == 0, halves[1], halves[0])

    def relay(g, i):
        pair_copy(g, i).wait_recv()
        start_away(g, i, 1)
        start_near(g, i, 1)

    def wait_far(g, block_at, only=None):
        if block_at < 0:
            relayed, low = ((1, 0), (1, block), (0, block))[-1 - block_at]
        else:
            relayed, low = ((0, 0), (0, block), (1, block))[block_at - 4]
        for i, (start, count) in enumerate(parts[g]):
            if low <= start < low + block and (only is None or i in only):
                @pl.when(has_near if block_at < 0 else has_away)
                def _():
                    (away_copy if block_at < 0 else near_copy)(g, i, relayed).wait_recv()

    units = ((2, 0, block), (3, 0, block // 2), (3, block // 2, block - block // 2), (1, 0, block), (0, 0, block))

    def place(u):
        m, low, count = units[u]
        return m + y * (3 - 2 * m), low + y * (block - 2 * low - count), count

    def image_unit(g, u, lags, fresh=False):
        chunk, low, count = place(u)
        image_chunk(g, chunk, lags, fresh, low, count)

    def image_chunk(g, chunk, lags, fresh=False, low=0, count=block):
        @pl.loop(low, low + count)
        def _(x):
            at = HALF + chunk * block + x
            totals = [None] * ANGLES
            for h in lags:
                reach = depth_out + (ANGLES - 1) * h // ANGLES
                tall = min(rows, -(-reach // 8) * 8)
                value = window[g, 0, at - h, :tall] * window[g, 1, at + h, :tall]
                if h:
                    value = value + window[g, 0, at + h, :tall] * window[g, 1, at - h, :tall]
                if h > 1:
                    product[h % 4, :tall] = value
                for a in range(ANGLES):
                    moved = a * h // ANGLES
                    piece = product[h % 4, moved : moved + depth_out] if moved else value[:depth_out]
                    totals[a] = piece if totals[a] is None else totals[a] + piece
            for i in range(ANGLES // 2):
                even, odd = totals[2 * i], totals[2 * i + 1]
                low = first_half[:depth_out]
                folded = jnp.where(low, even, odd)
                folded = folded + pltpu.roll(jnp.where(low, odd, even), lanes, 1)
                if not fresh:
                    folded = folded + image[chunk, i, x]
                image[chunk, i, x] = folded

    def core_copy(u):
        chunk, low, count = place(u)
        return pltpu.make_async_remote_copy(
            src_ref=image.at[chunk, pl.ds(packs * other, packs), pl.ds(low, count)],
            dst_ref=from_core.at[chunk, :, pl.ds(low, count)],
            send_sem=core_send.at[u],
            recv_sem=core_recv.at[u],
            device_id={"shot": other},
            device_id_type=MESH,
        )

    def out_copy(u):
        chunk, low, count = place(u)
        j = chunk - 2 * (1 - y)
        return pltpu.make_async_remote_copy(
            src_ref=summed.at[j, :, pl.ds(low, count)],
            dst_ref=from_pair.at[j, :, pl.ds(low, count)],
            send_sem=out_send.at[u],
            recv_sem=out_recv.at[u],
            device_id={"gx": pair},
            device_id_type=MESH,
        )

    def store_copy(j):
        kept = pl.ds(block * j, block)
        return pltpu.make_async_copy(result.at[:, kept], out.at[:, kept], store_sem.at[j])

    def pass_on(u):
        chunk, low, count = place(u)
        j = chunk - 2 * (1 - y)
        core_copy(u).wait_recv()

        @pl.loop(low, low + count)
        def _(x):
            for i in range(packs):
                summed[j, i, x] = image[chunk, packs * core + i, x] + from_core[chunk, i, x]

        out_copy(u).start()

    def finish(u, others):
        chunk, _, _ = place(u)
        j = chunk - 2 * y
        core_copy(u).wait_recv()
        for w in others:
            out_copy(w).wait_recv()

        @pl.loop(0, block)
        def _(x):
            low = first_half[:depth_out]
            for i in range(packs):
                mine = image[chunk, packs * core + i, x] + from_core[chunk, i, x]
                theirs = from_pair[j, i, x]
                left = jnp.where(y == 0, mine, theirs) * scale
                right = jnp.where(y == 0, theirs, mine) * scale
                result[2 * i, j * block + x] = jnp.where(low, left, pltpu.roll(right, lanes, 1))
                result[2 * i + 1, j * block + x] = jnp.where(low, pltpu.roll(left, lanes, 1), right)

        store_copy(j).start()

    loads[0].wait()
    loads[1].wait()
    send_halo(0)
    for load in loads[2:]:
        load.wait()
    mirror_steps(0, block - 1, block)
    part_steps(1, 0, 0)
    pack(0, 0)
    pair_copy(0, 0).start()
    start_away(0, 0, 0)
    start_near(0, 0, 0)
    mirror_steps(0, 1, block - 2)
    part_steps(1, 0, 1)
    pack(0, 1)
    wait_halo(0)
    both_sides(0, 0, 1)
    send_halo(1)
    pair_copy(0, 1).start()
    start_near(0, 1, 0)
    steps(2, 3, planes - 3)
    steps(3, 4, planes - 4)
    for i in range(3):
        pack(1, i)
    start_away(1, 0, 0)
    relay(0, 0)
    wait_halo(1)
    both_sides(1, 0, 2)
    send_halo(2)
    for i in (2, 3):
        pack(0, i)
        pair_copy(0, i).start()
        start_away(0, i, 0)
        start_near(0, i, 0)
    start_away(1, 1, 0)
    both_sides(2, 1, 3)
    relay(0, 1)
    wait_halo(2)
    both_sides(2, 0, 1)
    send_halo(3)
    for i in (2, 0, 1):
        pair_copy(1, i).start()
    both_sides(3, 1, 4)
    relay(0, 2)
    relay(0, 3)
    for i in (2, 0, 1):
        start_near(1, i, 0)
    near, far = range(block + 1), range(2 * block + 1, HALF + 1)
    rest, most = range(block + 1, HALF + 1), range(2 * block + 1)

    image_chunk(0, 1, near, True)
    pass
    image_chunk(0, 2, near, True)
    wait_halo(3)
    both_sides(3, 0, 1)
    for i in (3, 4):
        pack(1, i)
        pair_copy(1, i).start()
        start_away(1, i, 0)
        start_near(1, i, 0)
    for at in (-3, -2, -1, 4, 5, 6):
        wait_far(0, at)
    image_chunk(0, 1, rest)
    relay(1, 2)
    image_chunk(0, 2, rest)
    for i in range(2):
        pair_copy(1, i).wait_recv()
        start_away(1, i, 1)
    image_chunk(0, 0, range(HALF + 1), True)
    relay(1, 3)
    image_chunk(0, 3, range(HALF + 1), True)
    relay(1, 4)
    for i in (1, 0):
        start_near(1, i, 1)
    wait_far(1, 4)
    wait_far(1, 5)
    wait_far(1, -1)
    image_unit(1, 0, range(HALF + 1))
    core_copy(0).start()
    image_unit(1, 1, most)
    image_unit(1, 2, most)
    pass_on(0)
    image_unit(1, 3, most)
    image_unit(1, 4, near)
    wait_far(1, 6, (4,))
    image_unit(1, 1, far)
    core_copy(1).start()
    wait_far(1, 6, (0, 1))
    image_unit(1, 2, far)
    core_copy(2).start()
    pass_on(1)
    wait_far(1, -2)
    wait_far(1, -3)
    image_unit(1, 3, far)
    core_copy(3).start()
    pass_on(2)
    image_unit(1, 4, rest)
    core_copy(4).start()
    finish(3, (0,))
    finish(4, (1, 2))
    for j in range(2):
        store_copy(j).wait()

    for t in range(STEPS):
        each_halo(t, lambda c: c.wait_send(), lambda c: c.wait_send())
        if t in by_pair:
            @pl.when(has_away)
            def _():
                passed_copy(t).wait_send()

    for g in range(IMAGES):
        for i in range(len(parts[g])):
            pair_copy(g, i).wait_send()
            for relayed in range(2):
                if relayed or inner(g, i):
                    @pl.when(has_away)
                    def _():
                        away_copy(g, i, relayed).wait_send()
                if not relayed or inner(g, i):
                    @pl.when(has_near)
                    def _():
                        near_copy(g, i, relayed).wait_send()

    for u in range(len(units)):
        core_copy(u).wait_send()
    for u in range(3):
        out_copy(u).wait_send()


def solution(mesh):
    n = mesh.shape["gx"]
    cores = mesh.shape["shot"]

    def local(src_now, src_prev, rec_now, rec_prev, courant_sq, wavelet, traces, positions):
        shots, planes, depth, width = src_now.shape
        depth_out = depth // 2
        reach = depth_out + (ANGLES - 1) * HALF // ANGLES
        rows = min(depth, -(-(reach + STEPS - 1) // 8) * 8)
        block = planes // 2
        assert n % 2 == 0 and cores == 2 and shots == 2 and 3 * block == HALF and width % 2 == 0
        angles_out = ANGLES // cores
        scale = 1.0 / math.sqrt(LAGS * shots * cores * IMAGES)
        smem = pl.BlockSpec(memory_space=pltpu.SMEM)
        hbm = pl.BlockSpec(memory_space=pl.ANY)
        f32 = jnp.float32
        dma = pltpu.SemaphoreType.DMA
        return pl.pallas_call(
            functools.partial(kernel, n, scale, rows, reach),
            out_shape=jax.ShapeDtypeStruct((angles_out, planes, depth_out, width), f32),
            in_specs=[smem] * 3 + [hbm] * 5,
            out_specs=hbm,
            scratch_shapes=[
                pltpu.VMEM((STEPS + 2, 2, shots, planes + 2, depth, width), f32),
                pltpu.VMEM((planes, depth, width), f32),
                pltpu.VMEM((IMAGES, 2, 2 * planes + 2 * HALF, rows, width), f32),
                pltpu.VMEM((IMAGES, 2, planes, rows, width), f32),
                pltpu.VMEM((4, ANGLES // 2, block, depth_out, width), f32),
                pltpu.VMEM((4, angles_out // 2, block, depth_out, width), f32),
                pltpu.VMEM((2, angles_out // 2, block, depth_out, width), f32),
                pltpu.VMEM((2, angles_out // 2, block, depth_out, width), f32),
                pltpu.VMEM((4, rows, width), f32),
                pltpu.VMEM((2, 2, shots, depth, width), f32),
                pltpu.VMEM((angles_out, planes, depth_out, width), f32),
                dma((5,)),
                dma((2,)),
                dma((STEPS, 2)),
                dma((STEPS, 2)),
                dma((IMAGES, 5)),
                dma((IMAGES, 5)),
                dma((IMAGES, 5, 2)),
                dma((IMAGES, 5, 2)),
                dma((IMAGES, 5, 2)),
                dma((IMAGES, 5, 2)),
                dma((2, 2)),
                dma((2, 2)),
                dma((5,)),
                dma((5,)),
                dma((3,)),
                dma((3,)),
            ],
            compiler_params=pltpu.CompilerParams(
                collective_id=0, has_side_effects=True, vmem_limit_bytes=60 * 1024 * 1024
            ),
        )(positions, wavelet, traces, src_now, src_prev, rec_now, rec_prev, courant_sq)

    placed = (
        P(("groups", "shot"), "gx", None, None),
        P(("groups", "shot"), "gx", None, None),
        P(("groups", "shot"), "gx", None, None),
        P(("groups", "shot"), "gx", None, None),
        P(("groups", "gx"), None, None),
        P(("groups", "shot"), None),
        P(("groups", "shot"), None, "gx"),
        P(("groups", "shot"), None),
    )
    return jax.shard_map(
        local,
        mesh=mesh,
        in_specs=placed,
        out_specs=P(("groups", "shot"), "gx", None, None),
        check_vma=False,
    )
```

```python
import functools
import math

import jax
import jax.numpy as jnp
import numpy as np
from jax import lax
from jax.experimental import pallas as pl
from jax.experimental.pallas import tpu as pltpu
from jax.sharding import PartitionSpec as P

STEPS = 4
IMAGES = 2
LAGS = 49
ANGLES = 8
HALF = (LAGS - 1) // 2
MESH = pl.DeviceIdType.MESH


def lag_groups(block):
    edges = (-1, block, 2 * block, HALF)
    return [range(low + 1, high + 1) for low, high in zip(edges, edges[1:])]


def lag_rows(h, last, depth_out, rows):
    def kept(h):
        return -(-(depth_out + (ANGLES - 1) * h // ANGLES) // 8) * 8

    pair = h + 1 if last[0] % 2 == h % 2 else h - 1
    if pair > last[-1]:
        return min(rows, -(-kept(h) // 16) * 16)
    if (kept(h) + kept(pair)) % 16:
        return max(kept(h), kept(pair))
    return kept(h)


def slant_matrix(group, depth_out, rows):
    talls = [lag_rows(h, group, depth_out, rows) for h in group]
    total = sum(talls)
    ones = np.zeros((ANGLES * depth_out, 2 * total), np.float32)
    at = 0
    z = np.arange(depth_out)
    for h, tall in zip(group, talls):
        for a in range(ANGLES):
            for part in range(2):
                ones[a * depth_out + z, part * total + at + z + a * h // ANGLES] = 1.0
        at += tall
    return ones


def kernel(
    n,
    scale,
    rows,
    sent,
    positions,
    wavelet,
    traces,
    src_now,
    src_prev,
    rec_now,
    rec_prev,
    courant_hbm,
    near_hbm,
    middle_hbm,
    far_hbm,
    out,
    level,
    courant,
    window,
    outgoing,
    image,
    from_core,
    summed,
    from_pair,
    near_ones,
    middle_ones,
    far_ones,
    near_stack,
    middle_stack,
    far_stack,
    result,
    load_sem,
    store_sem,
    halo_send,
    halo_recv,
    pair_send,
    pair_recv,
    away_send,
    away_recv,
    near_send,
    near_recv,
    core_send,
    core_recv,
    out_send,
    out_recv,
):
    planes, depth, width = courant.shape
    block = planes // 2
    shots = src_now.shape[0]
    depth_out = out.shape[2]
    packs = from_core.shape[1]
    lanes = width // 2
    me = lax.axis_index("gx")
    core = lax.axis_index("shot")
    y = lax.rem(me, 2)
    pair = me + 1 - 2 * y
    other = 1 - core
    has_below = me >= 2
    has_above = me < n - 2
    has_away = ((y == 0) & has_above) | ((y == 1) & has_below)
    has_near = ((y == 0) & has_below) | ((y == 1) & has_above)
    parts = [
        ((block, block - 2), (2, block - 2), (planes - 2, 2), (0, 2)),
        ((block, 2), (block + 2, 2), (4, block - 4), (0, 4), (planes - 4, 4)),
    ]

    loads = []
    for i, (ref, k, f) in enumerate(
        ((src_now, 1, 0), (rec_now, 1, 1), (src_prev, 0, 0), (rec_prev, 0, 1))
    ):
        loads.append(
            pltpu.make_async_copy(ref, level.at[k, f, :, pl.ds(1, planes)], load_sem.at[i])
        )
    loads.append(pltpu.make_async_copy(courant_hbm, courant, load_sem.at[4]))
    for load in loads:
        load.start()
    ones = (near_ones, middle_ones, far_ones)
    stacks = (near_stack, middle_stack, far_stack)
    matrices = [
        pltpu.make_async_copy(ref, ones[k], load_sem.at[5 + k])
        for k, ref in enumerate((near_hbm, middle_hbm, far_hbm))
    ]
    for load in matrices:
        load.start()

    barrier = pltpu.get_barrier_semaphore()
    for step in (-2, -1, 1, 2):
        there = me + step

        @pl.when((there >= 0) & (there < n))
        def _():
            pl.semaphore_signal(barrier, inc=1, device_id={"gx": there}, device_id_type=MESH)

    pl.semaphore_signal(barrier, inc=1, device_id={"shot": other}, device_id_type=MESH)

    edge = jnp.zeros((rows, width), jnp.float32)
    full = jnp.zeros((depth, width), jnp.float32)

    @pl.when(me == 0)
    def _():
        for k in range(1, STEPS + 1):
            for f in range(2):
                for s in range(shots):
                    level[k, f, s, 0] = full

    @pl.when(me == n - 1)
    def _():
        for k in range(1, STEPS + 1):
            for f in range(2):
                for s in range(shots):
                    level[k, f, s, planes + 1] = full

    @pl.when(jnp.logical_not(has_below))
    def _():
        @pl.loop(0, HALF)
        def _(q):
            for g in range(IMAGES):
                for f in range(2):
                    window[g, f, q] = edge

    @pl.when(jnp.logical_not(has_above))
    def _():
        @pl.loop(0, HALF)
        def _(q):
            for g in range(IMAGES):
                for f in range(2):
                    window[g, f, HALF + 2 * planes + q] = edge

    peers = jnp.minimum(me, 2) + jnp.minimum(n - 1 - me, 2) + 1
    pl.semaphore_wait(barrier, peers)

    def halo(t, side):
        height = min(depth, sent + STEPS - 1 - t)
        kept = pl.ds(0, height)
        source, target = (planes, 0) if side == 0 else (1, planes + 1)
        return pltpu.make_async_remote_copy(
            src_ref=level.at[1 + t, :, :, source, kept],
            dst_ref=level.at[1 + t, :, :, target, kept],
            send_sem=halo_send.at[t, side],
            recv_sem=halo_recv.at[t, side],
            device_id={"gx": me + 1 if side == 0 else me - 1},
            device_id_type=MESH,
        )

    def send_halo(t):
        @pl.when(me < n - 1)
        def _():
            halo(t, 0).start()

        @pl.when(me > 0)
        def _():
            halo(t, 1).start()

    def wait_halo(t):
        @pl.when(me > 0)
        def _():
            halo(t, 0).wait_recv()

        @pl.when(me < n - 1)
        def _():
            halo(t, 1).wait_recv()

    z_row = lax.broadcasted_iota(jnp.int32, (rows, width), 0)
    y_lane = lax.broadcasted_iota(jnp.int32, (rows, width), 1)
    first = me * planes

    def plane_step(t, x):
        speed = courant[x - 1, :rows]
        tall = depth if t == 0 else rows
        for s in range(shots):
            for f in range(2):
                now_tall = level[1 + t, f, s, x, :tall]
                now = now_tall[:rows]
                low = level[1 + t, f, s, x - 1, :rows]
                high = level[1 + t, f, s, x + 1, :rows]
                zeros = jnp.zeros((1, width), jnp.float32)
                deeper = jnp.concatenate([now_tall[1:], zeros], axis=0)[:rows]
                shallower = jnp.concatenate([zeros, now[: rows - 1]], axis=0)
                left = jnp.where(y_lane == 0, 0.0, pltpu.roll(now, 1, 1))
                right = jnp.where(y_lane == width - 1, 0.0, pltpu.roll(now, width - 1, 1))
                beside = low + high + deeper + shallower + left + right
                nxt = 2.0 * now - level[t, f, s, x, :rows] + speed * (beside - 6.0 * now)
                if f == 0:
                    amount = jnp.where(first + x - 1 == positions[s, 0], wavelet[s, t], 0.0)
                    hit = (z_row == positions[s, 2]) & (y_lane == positions[s, 1])
                else:
                    amount = traces[s, STEPS - 1 - t, x - 1]
                    hit = (z_row == 0) & (y_lane == positions[s, 3])
                level[2 + t, f, s, x, :rows] = nxt + jnp.where(hit, amount, 0.0)

    def steps(t, low, high):
        @pl.loop(low + 1, high + 1)
        def _(x):
            plane_step(t, x)

    def both_sides(t, low, high):
        count = high - low

        @pl.loop(0, 2 * count)
        def _(i):
            side = i // count
            x = low + i - side * count
            plane_step(t, 1 + x + side * (planes - 1 - 2 * x))

    def begin(g, i, yy):
        low, count = parts[g][i]
        return low + yy * (planes - 2 * low - count)

    def mirror_steps(t, low, count):
        at = low + y * (planes - 2 * low - count)

        @pl.loop(0, count)
        def _(j):
            plane_step(t, 1 + at + j)

    def part_steps(t, g, i):
        at = begin(g, i, y)

        @pl.loop(0, parts[g][i][1])
        def _(j):
            plane_step(t, 1 + at + j)

    def pair_copy(g, i):
        at = begin(g, i, y)
        count = parts[g][i][1]
        return pltpu.make_async_remote_copy(
            src_ref=outgoing.at[g, :, pl.ds(at, count), pl.ds(0, sent)],
            dst_ref=window.at[g, :, pl.ds(HALF + planes * y + at, count), pl.ds(0, sent)],
            send_sem=pair_send.at[g, i],
            recv_sem=pair_recv.at[g, i],
            device_id={"gx": pair},
            device_id_type=MESH,
        )

    up_from, down_to = -block, HALF + 2 * planes

    def away_copy(g, i, relayed):
        yy = 1 - y if relayed else y
        at = planes * yy + begin(g, i, yy)
        count = parts[g][i][1]
        return pltpu.make_async_remote_copy(
            src_ref=window.at[g, :, pl.ds(HALF + at, count), pl.ds(0, sent)],
            dst_ref=window.at[
                g, :, pl.ds(at + up_from + y * (down_to - up_from), count), pl.ds(0, sent)
            ],
            send_sem=away_send.at[g, i, relayed],
            recv_sem=away_recv.at[g, i, relayed],
            device_id={"gx": me + 2 - 4 * y},
            device_id_type=MESH,
        )

    def near_copy(g, i, relayed):
        yy = 1 - y if relayed else y
        at = planes * yy + begin(g, i, yy)
        count = parts[g][i][1]
        return pltpu.make_async_remote_copy(
            src_ref=window.at[g, :, pl.ds(HALF + at, count), pl.ds(0, sent)],
            dst_ref=window.at[
                g, :, pl.ds(at + down_to + y * (up_from - down_to), count), pl.ds(0, sent)
            ],
            send_sem=near_send.at[g, i, relayed],
            recv_sem=near_recv.at[g, i, relayed],
            device_id={"gx": me - 2 + 4 * y},
            device_id_type=MESH,
        )

    def inner(g, i):
        return parts[g][i][0] >= block

    def start_away(g, i, relayed):
        if relayed or inner(g, i):
            @pl.when(has_away)
            def _():
                away_copy(g, i, relayed).start()

    def start_near(g, i, relayed):
        if not relayed or inner(g, i):
            @pl.when(has_near)
            def _():
                near_copy(g, i, relayed).start()

    first_half = y_lane < lanes

    def pack(g, i):
        at = begin(g, i, y)

        @pl.loop(0, parts[g][i][1])
        def _(j):
            x = at + j
            for f in range(2):
                one = level[2 * g + 3, f, 0, 1 + x, :rows]
                two = level[2 * g + 3, f, 1, 1 + x, :rows]
                halves = (
                    jnp.where(first_half, one, pltpu.roll(two, lanes, 1)),
                    jnp.where(first_half, pltpu.roll(one, lanes, 1), two),
                )
                window[g, f, HALF + planes * y + x] = jnp.where(y == 0, halves[0], halves[1])
                outgoing[g, f, x] = jnp.where(y == 0, halves[1], halves[0])

    def relay(g, i):
        pair_copy(g, i).wait_recv()
        start_away(g, i, 1)
        start_near(g, i, 1)

    def wait_far(g, block_at, only=None):
        if block_at < 0:
            relayed, low = ((1, 0), (1, block), (0, block))[-1 - block_at]
        else:
            relayed, low = ((0, 0), (0, block), (1, block))[block_at - 4]
        for i, (start, count) in enumerate(parts[g]):
            if low <= start < low + block and (only is None or i in only):
                @pl.when(has_near if block_at < 0 else has_away)
                def _():
                    (away_copy if block_at < 0 else near_copy)(g, i, relayed).wait_recv()

    units = ((2, 0, block), (3, 0, block // 2), (3, block // 2, block - block // 2), (1, 0, block), (0, 0, block))

    def place(u):
        m, low, count = units[u]
        return m + y * (3 - 2 * m), low + y * (block - 2 * low - count), count

    def image_unit(g, u, lags, fresh=False):
        chunk, low, count = place(u)
        image_chunk(g, chunk, lags, fresh, low, count)

    groups = lag_groups(block)
    low_half = lax.broadcasted_iota(jnp.int32, (8, width), 1) < lanes
    low_rows = [
        jnp.concatenate([low_half] * (tall // 8), axis=0) for tall in range(8, rows + 8, 8)
    ]
    known = lax.broadcasted_iota(jnp.int32, (8, width), 0) < sent - (rows - 8)

    def summed_product(g, at, h, tall):
        def one(at):
            value = window[g, 0, at - h, :tall] * window[g, 1, at + h, :tall]
            if h:
                value = value + window[g, 0, at + h, :tall] * window[g, 1, at - h, :tall]
            return value

        low = low_rows[tall // 8 - 1]
        even, odd = one(at), one(at + 1)
        folded = jnp.where(low, even, odd) + pltpu.roll(jnp.where(low, odd, even), lanes, 1)
        if tall == rows:
            last = jnp.where(known, folded[rows - 8 :], 0.0)
            folded = jnp.concatenate([folded[: rows - 8], last], axis=0)
        return folded

    def image_chunk(g, chunk, lags, fresh=False, low=0, count=block):
        used = [k for k in range(3) if groups[k][0] in lags]

        @pl.loop(0, count // 4)
        def _(q):
            x = low + 4 * q
            for k in used:
                half_rows = stacks[k].shape[0] // 2

                @pl.loop(0, 2)
                def _(j, k=k, half_rows=half_rows):
                    at = HALF + chunk * block + x + 2 * j
                    columns = pl.ds(pl.multiple_of(j * width, width), width)
                    top = 0
                    group = groups[k]
                    for i in range(0, len(group), 2):
                        both = [
                            summed_product(g, at, h, lag_rows(h, group, depth_out, rows))
                            for h in group[i : i + 2]
                        ]
                        value = jnp.concatenate(both, axis=0) if len(both) > 1 else both[0]
                        high = value.astype(jnp.bfloat16)
                        rest_of = (value - high.astype(jnp.float32)).astype(jnp.bfloat16)
                        tall = value.shape[0]
                        stacks[k][top : top + tall, columns] = high
                        stacks[k][half_rows + top : half_rows + top + tall, columns] = rest_of
                        top += tall

            total = None
            for k in used:
                part = jnp.dot(ones[k][...], stacks[k][...], preferred_element_type=jnp.float32)
                total = part if total is None else total + part
            for j in range(2):
                for a in range(ANGLES):
                    piece = total[a * depth_out : (a + 1) * depth_out, j * width : (j + 1) * width]
                    if not fresh:
                        piece = piece + image[chunk, a, x // 2 + j]
                    image[chunk, a, x // 2 + j] = piece

    def core_copy(u):
        chunk, low, count = place(u)
        return pltpu.make_async_remote_copy(
            src_ref=image.at[chunk, pl.ds(packs * other, packs), pl.ds(low // 2, count // 2)],
            dst_ref=from_core.at[chunk, :, pl.ds(low // 2, count // 2)],
            send_sem=core_send.at[u],
            recv_sem=core_recv.at[u],
            device_id={"shot": other},
            device_id_type=MESH,
        )

    def out_copy(u):
        chunk, low, count = place(u)
        j = chunk - 2 * (1 - y)
        return pltpu.make_async_remote_copy(
            src_ref=summed.at[j, :, pl.ds(low // 2, count // 2)],
            dst_ref=from_pair.at[j, :, pl.ds(low // 2, count // 2)],
            send_sem=out_send.at[u],
            recv_sem=out_recv.at[u],
            device_id={"gx": pair},
            device_id_type=MESH,
        )

    def store_copy(j):
        kept = pl.ds(block * j, block)
        return pltpu.make_async_copy(result.at[:, kept], out.at[:, kept], store_sem.at[j])

    def pass_on(u):
        chunk, low, count = place(u)
        j = chunk - 2 * (1 - y)
        core_copy(u).wait_recv()

        @pl.loop(low // 2, (low + count) // 2)
        def _(x):
            for i in range(packs):
                summed[j, i, x] = image[chunk, packs * core + i, x] + from_core[chunk, i, x]

        out_copy(u).start()

    def finish(u, others):
        chunk, _, _ = place(u)
        j = chunk - 2 * y
        core_copy(u).wait_recv()
        for w in others:
            out_copy(w).wait_recv()

        @pl.loop(0, block // 2)
        def _(x):
            low = first_half[:depth_out]
            for i in range(packs):
                mine = image[chunk, packs * core + i, x] + from_core[chunk, i, x]
                theirs = from_pair[j, i, x]
                left = jnp.where(y == 0, mine, theirs) * scale
                right = jnp.where(y == 0, theirs, mine) * scale
                result[i, j * block + 2 * x] = jnp.where(low, left, pltpu.roll(right, lanes, 1))
                second = jnp.where(low, pltpu.roll(left, lanes, 1), right)
                result[i, j * block + 2 * x + 1] = second

        store_copy(j).start()

    loads[0].wait()
    loads[1].wait()
    send_halo(0)
    for load in loads[2:]:
        load.wait()
    mirror_steps(0, block - 1, block)
    part_steps(1, 0, 0)
    pack(0, 0)
    pair_copy(0, 0).start()
    start_away(0, 0, 0)
    start_near(0, 0, 0)
    mirror_steps(0, 1, block - 2)
    part_steps(1, 0, 1)
    pack(0, 1)
    wait_halo(0)
    both_sides(0, 0, 1)
    send_halo(1)
    pair_copy(0, 1).start()
    start_near(0, 1, 0)
    steps(2, 3, planes - 3)
    steps(3, 4, planes - 4)
    for i in range(3):
        pack(1, i)
    start_away(1, 0, 0)
    relay(0, 0)
    wait_halo(1)
    both_sides(1, 0, 2)
    send_halo(2)
    for i in (2, 3):
        pack(0, i)
        pair_copy(0, i).start()
        start_away(0, i, 0)
        start_near(0, i, 0)
    start_away(1, 1, 0)
    both_sides(2, 1, 3)
    relay(0, 1)
    wait_halo(2)
    both_sides(2, 0, 1)
    send_halo(3)
    for i in (2, 0, 1):
        pair_copy(1, i).start()
    both_sides(3, 1, 4)
    relay(0, 2)
    relay(0, 3)
    for i in (2, 0, 1):
        start_near(1, i, 0)
    near, far = range(block + 1), range(2 * block + 1, HALF + 1)
    rest, most = range(block + 1, HALF + 1), range(2 * block + 1)

    for load in matrices:
        load.wait()
    image_chunk(0, 1, near, True)
    image_chunk(0, 2, near, True)
    wait_halo(3)
    both_sides(3, 0, 1)
    for i in (3, 4):
        pack(1, i)
        pair_copy(1, i).start()
        start_away(1, i, 0)
        start_near(1, i, 0)
    for at in (-3, -2, -1, 4, 5, 6):
        wait_far(0, at)
    image_chunk(0, 1, rest)
    relay(1, 2)
    image_chunk(0, 2, rest)
    for i in range(2):
        pair_copy(1, i).wait_recv()
        start_away(1, i, 1)
    image_chunk(0, 0, range(HALF + 1), True)
    relay(1, 3)
    image_chunk(0, 3, range(HALF + 1), True)
    relay(1, 4)
    for i in (1, 0):
        start_near(1, i, 1)
    wait_far(1, 4)
    wait_far(1, 5)
    wait_far(1, -1)
    image_unit(1, 0, range(HALF + 1))
    core_copy(0).start()
    image_unit(1, 1, most)
    image_unit(1, 2, most)
    pass_on(0)
    image_unit(1, 3, most)
    image_unit(1, 4, near)
    wait_far(1, 6, (4,))
    image_unit(1, 1, far)
    core_copy(1).start()
    wait_far(1, 6, (0, 1))
    image_unit(1, 2, far)
    core_copy(2).start()
    pass_on(1)
    wait_far(1, -2)
    wait_far(1, -3)
    image_unit(1, 3, far)
    core_copy(3).start()
    pass_on(2)
    image_unit(1, 4, rest)
    core_copy(4).start()
    finish(3, (0,))
    finish(4, (1, 2))
    for j in range(2):
        store_copy(j).wait()

    for t in range(STEPS):
        @pl.when(me < n - 1)
        def _():
            halo(t, 0).wait_send()

        @pl.when(me > 0)
        def _():
            halo(t, 1).wait_send()

    for g in range(IMAGES):
        for i in range(len(parts[g])):
            pair_copy(g, i).wait_send()
            for relayed in range(2):
                if relayed or inner(g, i):
                    @pl.when(has_away)
                    def _():
                        away_copy(g, i, relayed).wait_send()
                if not relayed or inner(g, i):
                    @pl.when(has_near)
                    def _():
                        near_copy(g, i, relayed).wait_send()

    for u in range(len(units)):
        core_copy(u).wait_send()
    for u in range(3):
        out_copy(u).wait_send()


def solution(mesh):
    n = mesh.shape["gx"]
    cores = mesh.shape["shot"]

    def local(src_now, src_prev, rec_now, rec_prev, courant_sq, wavelet, traces, positions):
        shots, planes, depth, width = src_now.shape
        depth_out = depth // 2
        reach = depth_out + (ANGLES - 1) * HALF // ANGLES
        rows = min(depth, -(-(reach + STEPS - 1) // 8) * 8)
        block = planes // 2
        assert n % 2 == 0 and cores == 2 and shots == 2 and 3 * block == HALF and block % 4 == 0 and width % 2 == 0
        angles_out = ANGLES // cores
        scale = 1.0 / math.sqrt(LAGS * shots * cores * IMAGES)
        smem = pl.BlockSpec(memory_space=pltpu.SMEM)
        hbm = pl.BlockSpec(memory_space=pl.ANY)
        matrices = [
            jnp.asarray(slant_matrix(group, depth_out, rows), jnp.bfloat16)
            for group in lag_groups(block)
        ]
        f32 = jnp.float32
        dma = pltpu.SemaphoreType.DMA
        return pl.pallas_call(
            functools.partial(kernel, n, scale, rows, reach),
            out_shape=jax.ShapeDtypeStruct((angles_out, planes, depth_out, width), f32),
            in_specs=[smem] * 3 + [hbm] * 8,
            out_specs=hbm,
            scratch_shapes=[
                pltpu.VMEM((STEPS + 2, 2, shots, planes + 2, depth, width), f32),
                pltpu.VMEM((planes, depth, width), f32),
                pltpu.VMEM((IMAGES, 2, 2 * planes + 2 * HALF, rows, width), f32),
                pltpu.VMEM((IMAGES, 2, planes, rows, width), f32),
                pltpu.VMEM((4, ANGLES, block // 2, depth_out, width), f32),
                pltpu.VMEM((4, angles_out, block // 2, depth_out, width), f32),
                pltpu.VMEM((2, angles_out, block // 2, depth_out, width), f32),
                pltpu.VMEM((2, angles_out, block // 2, depth_out, width), f32),
                *[pltpu.VMEM(m.shape, jnp.bfloat16) for m in matrices],
                *[pltpu.VMEM((m.shape[1], 2 * width), jnp.bfloat16) for m in matrices],
                pltpu.VMEM((angles_out, planes, depth_out, width), f32),
                dma((8,)),
                dma((2,)),
                dma((STEPS, 2)),
                dma((STEPS, 2)),
                dma((IMAGES, 5)),
                dma((IMAGES, 5)),
                dma((IMAGES, 5, 2)),
                dma((IMAGES, 5, 2)),
                dma((IMAGES, 5, 2)),
                dma((IMAGES, 5, 2)),
                dma((5,)),
                dma((5,)),
                dma((3,)),
                dma((3,)),
            ],
            compiler_params=pltpu.CompilerParams(
                collective_id=0, has_side_effects=True, vmem_limit_bytes=60 * 1024 * 1024
            ),
        )(positions, wavelet, traces, src_now, src_prev, rec_now, rec_prev, courant_sq, *matrices)

    placed = (
        P(("groups", "shot"), "gx", None, None),
        P(("groups", "shot"), "gx", None, None),
        P(("groups", "shot"), "gx", None, None),
        P(("groups", "shot"), "gx", None, None),
        P(("groups", "gx"), None, None),
        P(("groups", "shot"), None),
        P(("groups", "shot"), None, "gx"),
        P(("groups", "shot"), None),
    )
    return jax.shard_map(
        local,
        mesh=mesh,
        in_specs=placed,
        out_specs=P(("groups", "shot"), "gx", None, None),
        check_vma=False,
    )
```

```python
import functools
import math

import jax
import jax.numpy as jnp
import numpy as np
from jax import lax
from jax.experimental import pallas as pl
from jax.experimental.pallas import tpu as pltpu
from jax.sharding import PartitionSpec as P

STEPS = 4
IMAGES = 2
LAGS = 49
ANGLES = 8
HALF = (LAGS - 1) // 2
MESH = pl.DeviceIdType.MESH


def lag_groups(block):
    edges = (-1, block, 2 * block, HALF)
    return [range(low + 1, high + 1) for low, high in zip(edges, edges[1:])]


def lag_rows(h, last, depth_out, rows):
    def kept(h):
        return -(-(depth_out + (ANGLES - 1) * h // ANGLES) // 8) * 8

    pair = h + 1 if last[0] % 2 == h % 2 else h - 1
    if pair > last[-1]:
        return min(rows, -(-kept(h) // 16) * 16)
    if (kept(h) + kept(pair)) % 16:
        return max(kept(h), kept(pair))
    return kept(h)


def slant_matrix(group, depth_out, rows):
    talls = [lag_rows(h, group, depth_out, rows) for h in group]
    total = sum(talls)
    ones = np.zeros((ANGLES * depth_out, 2 * total), np.float32)
    at = 0
    z = np.arange(depth_out)
    for h, tall in zip(group, talls):
        for a in range(ANGLES):
            for part in range(2):
                ones[a * depth_out + z, part * total + at + z + a * h // ANGLES] = 1.0
        at += tall
    return ones


def kernel(
    n,
    scale,
    rows,
    sent,
    positions,
    wavelet,
    traces,
    src_now,
    src_prev,
    rec_now,
    rec_prev,
    courant_hbm,
    near_hbm,
    middle_hbm,
    far_hbm,
    out,
    level,
    courant,
    window,
    outgoing,
    image,
    from_core,
    summed,
    from_pair,
    near_ones,
    middle_ones,
    far_ones,
    near_stack,
    middle_stack,
    far_stack,
    result,
    load_sem,
    store_sem,
    halo_send,
    halo_recv,
    pair_send,
    pair_recv,
    away_send,
    away_recv,
    near_send,
    near_recv,
    core_send,
    core_recv,
    out_send,
    out_recv,
):
    planes, depth, width = courant.shape
    block = planes // 2
    shots = src_now.shape[0]
    depth_out = out.shape[2]
    packs = from_core.shape[1]
    lanes = width // 2
    me = lax.axis_index("gx")
    core = lax.axis_index("shot")
    y = lax.rem(me, 2)
    pair = me + 1 - 2 * y
    other = 1 - core
    has_below = me >= 2
    has_above = me < n - 2
    has_away = ((y == 0) & has_above) | ((y == 1) & has_below)
    has_near = ((y == 0) & has_below) | ((y == 1) & has_above)
    parts = [
        ((block, block - 2), (2, block - 2), (planes - 2, 2), (0, 2)),
        ((block, 2), (block + 2, 2), (4, block - 4), (0, 4), (planes - 4, 4)),
    ]

    loads = []
    for i, (ref, k, f) in enumerate(
        ((src_now, 1, 0), (rec_now, 1, 1), (src_prev, 0, 0), (rec_prev, 0, 1))
    ):
        loads.append(
            pltpu.make_async_copy(ref, level.at[k, f, :, pl.ds(1, planes)], load_sem.at[i])
        )
    loads.append(pltpu.make_async_copy(courant_hbm, courant, load_sem.at[4]))
    for load in loads:
        load.start()
    ones = (near_ones, middle_ones, far_ones)
    stacks = (near_stack, middle_stack, far_stack)
    matrices = [
        pltpu.make_async_copy(ref, ones[k], load_sem.at[5 + k])
        for k, ref in enumerate((near_hbm, middle_hbm, far_hbm))
    ]
    for load in matrices:
        load.start()

    barrier = pltpu.get_barrier_semaphore()
    for step in (-2, -1, 1, 2):
        there = me + step

        @pl.when((there >= 0) & (there < n))
        def _():
            pl.semaphore_signal(barrier, inc=1, device_id={"gx": there}, device_id_type=MESH)

    pl.semaphore_signal(barrier, inc=1, device_id={"shot": other}, device_id_type=MESH)

    edge = jnp.zeros((rows, width), jnp.float32)
    full = jnp.zeros((depth, width), jnp.float32)

    @pl.when(me == 0)
    def _():
        for k in range(1, STEPS + 1):
            for f in range(2):
                for s in range(shots):
                    level[k, f, s, 0] = full

    @pl.when(me == n - 1)
    def _():
        for k in range(1, STEPS + 1):
            for f in range(2):
                for s in range(shots):
                    level[k, f, s, planes + 1] = full

    @pl.when(jnp.logical_not(has_below))
    def _():
        @pl.loop(0, HALF)
        def _(q):
            for g in range(IMAGES):
                for f in range(2):
                    window[g, f, q] = edge

    @pl.when(jnp.logical_not(has_above))
    def _():
        @pl.loop(0, HALF)
        def _(q):
            for g in range(IMAGES):
                for f in range(2):
                    window[g, f, HALF + 2 * planes + q] = edge

    peers = jnp.minimum(me, 2) + jnp.minimum(n - 1 - me, 2) + 1
    pl.semaphore_wait(barrier, peers)

    def halo(t, side):
        height = min(depth, sent + STEPS - 1 - t)
        kept = pl.ds(0, height)
        source, target = (planes, 0) if side == 0 else (1, planes + 1)
        return pltpu.make_async_remote_copy(
            src_ref=level.at[1 + t, :, :, source, kept],
            dst_ref=level.at[1 + t, :, :, target, kept],
            send_sem=halo_send.at[t, side],
            recv_sem=halo_recv.at[t, side],
            device_id={"gx": me + 1 if side == 0 else me - 1},
            device_id_type=MESH,
        )

    def send_halo(t):
        @pl.when(me < n - 1)
        def _():
            halo(t, 0).start()

        @pl.when(me > 0)
        def _():
            halo(t, 1).start()

    def wait_halo(t):
        @pl.when(me > 0)
        def _():
            halo(t, 0).wait_recv()

        @pl.when(me < n - 1)
        def _():
            halo(t, 1).wait_recv()

    z_row = lax.broadcasted_iota(jnp.int32, (rows, width), 0)
    y_lane = lax.broadcasted_iota(jnp.int32, (rows, width), 1)
    first = me * planes

    def plane_step(t, x):
        speed = courant[x - 1, :rows]
        tall = depth if t == 0 else rows
        for s in range(shots):
            for f in range(2):
                now_tall = level[1 + t, f, s, x, :tall]
                now = now_tall[:rows]
                low = level[1 + t, f, s, x - 1, :rows]
                high = level[1 + t, f, s, x + 1, :rows]
                zeros = jnp.zeros((1, width), jnp.float32)
                deeper = jnp.concatenate([now_tall[1:], zeros], axis=0)[:rows]
                shallower = jnp.concatenate([zeros, now[: rows - 1]], axis=0)
                left = jnp.where(y_lane == 0, 0.0, pltpu.roll(now, 1, 1))
                right = jnp.where(y_lane == width - 1, 0.0, pltpu.roll(now, width - 1, 1))
                beside = low + high + deeper + shallower + left + right
                nxt = 2.0 * now - level[t, f, s, x, :rows] + speed * (beside - 6.0 * now)
                if f == 0:
                    amount = jnp.where(first + x - 1 == positions[s, 0], wavelet[s, t], 0.0)
                    hit = (z_row == positions[s, 2]) & (y_lane == positions[s, 1])
                else:
                    amount = traces[s, STEPS - 1 - t, x - 1]
                    hit = (z_row == 0) & (y_lane == positions[s, 3])
                level[2 + t, f, s, x, :rows] = nxt + jnp.where(hit, amount, 0.0)

    def steps(t, low, high):
        @pl.loop(low + 1, high + 1)
        def _(x):
            plane_step(t, x)

    def both_sides(t, low, high):
        count = high - low

        @pl.loop(0, 2 * count)
        def _(i):
            side = i // count
            x = low + i - side * count
            plane_step(t, 1 + x + side * (planes - 1 - 2 * x))

    def begin(g, i, yy):
        low, count = parts[g][i]
        return low + yy * (planes - 2 * low - count)

    def mirror_steps(t, low, count):
        at = low + y * (planes - 2 * low - count)

        @pl.loop(0, count)
        def _(j):
            plane_step(t, 1 + at + j)

    def part_steps(t, g, i):
        at = begin(g, i, y)

        @pl.loop(0, parts[g][i][1])
        def _(j):
            plane_step(t, 1 + at + j)

    def pair_copy(g, i):
        at = begin(g, i, y)
        count = parts[g][i][1]
        return pltpu.make_async_remote_copy(
            src_ref=outgoing.at[g, :, pl.ds(at, count), pl.ds(0, sent)],
            dst_ref=window.at[g, :, pl.ds(HALF + planes * y + at, count), pl.ds(0, sent)],
            send_sem=pair_send.at[g, i],
            recv_sem=pair_recv.at[g, i],
            device_id={"gx": pair},
            device_id_type=MESH,
        )

    up_from, down_to = -block, HALF + 2 * planes

    def away_copy(g, i, relayed):
        yy = 1 - y if relayed else y
        at = planes * yy + begin(g, i, yy)
        count = parts[g][i][1]
        return pltpu.make_async_remote_copy(
            src_ref=window.at[g, :, pl.ds(HALF + at, count), pl.ds(0, sent)],
            dst_ref=window.at[
                g, :, pl.ds(at + up_from + y * (down_to - up_from), count), pl.ds(0, sent)
            ],
            send_sem=away_send.at[g, i, relayed],
            recv_sem=away_recv.at[g, i, relayed],
            device_id={"gx": me + 2 - 4 * y},
            device_id_type=MESH,
        )

    def near_copy(g, i, relayed):
        yy = 1 - y if relayed else y
        at = planes * yy + begin(g, i, yy)
        count = parts[g][i][1]
        return pltpu.make_async_remote_copy(
            src_ref=window.at[g, :, pl.ds(HALF + at, count), pl.ds(0, sent)],
            dst_ref=window.at[
                g, :, pl.ds(at + down_to + y * (up_from - down_to), count), pl.ds(0, sent)
            ],
            send_sem=near_send.at[g, i, relayed],
            recv_sem=near_recv.at[g, i, relayed],
            device_id={"gx": me - 2 + 4 * y},
            device_id_type=MESH,
        )

    def inner(g, i):
        return parts[g][i][0] >= block

    def start_away(g, i, relayed):
        if relayed or inner(g, i):
            @pl.when(has_away)
            def _():
                away_copy(g, i, relayed).start()

    def start_near(g, i, relayed):
        if not relayed or inner(g, i):
            @pl.when(has_near)
            def _():
                near_copy(g, i, relayed).start()

    first_half = y_lane < lanes

    def pack(g, i):
        at = begin(g, i, y)

        @pl.loop(0, parts[g][i][1])
        def _(j):
            x = at + j
            for f in range(2):
                one = level[2 * g + 3, f, 0, 1 + x, :rows]
                two = level[2 * g + 3, f, 1, 1 + x, :rows]
                halves = (
                    jnp.where(first_half, one, pltpu.roll(two, lanes, 1)),
                    jnp.where(first_half, pltpu.roll(one, lanes, 1), two),
                )
                window[g, f, HALF + planes * y + x] = jnp.where(y == 0, halves[0], halves[1])
                outgoing[g, f, x] = jnp.where(y == 0, halves[1], halves[0])

    def relay(g, i):
        pair_copy(g, i).wait_recv()
        start_away(g, i, 1)
        start_near(g, i, 1)

    def wait_far(g, block_at, only=None):
        if block_at < 0:
            relayed, low = ((1, 0), (1, block), (0, block))[-1 - block_at]
        else:
            relayed, low = ((0, 0), (0, block), (1, block))[block_at - 4]
        for i, (start, count) in enumerate(parts[g]):
            if low <= start < low + block and (only is None or i in only):
                @pl.when(has_near if block_at < 0 else has_away)
                def _():
                    (away_copy if block_at < 0 else near_copy)(g, i, relayed).wait_recv()

    units = ((2, 0, block), (3, 0, block // 2), (3, block // 2, block - block // 2), (1, 0, block), (0, 0, block))

    def place(u):
        m, low, count = units[u]
        return m + y * (3 - 2 * m), low + y * (block - 2 * low - count), count

    def image_unit(g, u, lags, fresh=False):
        chunk, low, count = place(u)
        image_chunk(g, chunk, lags, fresh, low, count)

    groups = lag_groups(block)
    low_half = lax.broadcasted_iota(jnp.int32, (8, width), 1) < lanes
    low_rows = [
        jnp.concatenate([low_half] * (tall // 8), axis=0) for tall in range(8, rows + 8, 8)
    ]
    known = lax.broadcasted_iota(jnp.int32, (8, width), 0) < sent - (rows - 8)

    def summed_product(g, at, h, tall):
        def one(at):
            value = window[g, 0, at - h, :tall] * window[g, 1, at + h, :tall]
            if h:
                value = value + window[g, 0, at + h, :tall] * window[g, 1, at - h, :tall]
            return value

        low = low_rows[tall // 8 - 1]
        even, odd = one(at), one(at + 1)
        folded = jnp.where(low, even, odd) + pltpu.roll(jnp.where(low, odd, even), lanes, 1)
        if tall == rows:
            last = jnp.where(known, folded[rows - 8 :], 0.0)
            folded = jnp.concatenate([folded[: rows - 8], last], axis=0)
        return folded

    def image_chunk(g, chunk, lags, fresh=False, low=0, count=block):
        used = [k for k in range(3) if groups[k][0] in lags]

        @pl.loop(0, count // 4)
        def _(q):
            x = low + 4 * q
            total = None
            for k in used:
                half_rows = stacks[k].shape[0] // 2
                group = groups[k]
                for j in range(2):
                    at = HALF + chunk * block + x + 2 * j
                    columns = slice(j * width, (j + 1) * width)
                    top = 0
                    for i in range(0, len(group), 2):
                        both = [
                            summed_product(g, at, h, lag_rows(h, group, depth_out, rows))
                            for h in group[i : i + 2]
                        ]
                        value = jnp.concatenate(both, axis=0) if len(both) > 1 else both[0]
                        high = value.astype(jnp.bfloat16)
                        rest_of = (value - high.astype(jnp.float32)).astype(jnp.bfloat16)
                        tall = value.shape[0]
                        stacks[k][top : top + tall, columns] = high
                        stacks[k][half_rows + top : half_rows + top + tall, columns] = rest_of
                        top += tall
                part = jnp.dot(ones[k][...], stacks[k][...], preferred_element_type=jnp.float32)
                total = part if total is None else total + part
            for j in range(2):
                for a in range(ANGLES):
                    piece = total[a * depth_out : (a + 1) * depth_out, j * width : (j + 1) * width]
                    if not fresh:
                        piece = piece + image[chunk, a, x // 2 + j]
                    image[chunk, a, x // 2 + j] = piece

    def core_copy(u):
        chunk, low, count = place(u)
        return pltpu.make_async_remote_copy(
            src_ref=image.at[chunk, pl.ds(packs * other, packs), pl.ds(low // 2, count // 2)],
            dst_ref=from_core.at[chunk, :, pl.ds(low // 2, count // 2)],
            send_sem=core_send.at[u],
            recv_sem=core_recv.at[u],
            device_id={"shot": other},
            device_id_type=MESH,
        )

    def out_copy(u):
        chunk, low, count = place(u)
        j = chunk - 2 * (1 - y)
        return pltpu.make_async_remote_copy(
            src_ref=summed.at[j, :, pl.ds(low // 2, count // 2)],
            dst_ref=from_pair.at[j, :, pl.ds(low // 2, count // 2)],
            send_sem=out_send.at[u],
            recv_sem=out_recv.at[u],
            device_id={"gx": pair},
            device_id_type=MESH,
        )

    def store_copy(j):
        kept = pl.ds(block * j, block)
        return pltpu.make_async_copy(result.at[:, kept], out.at[:, kept], store_sem.at[j])

    def pass_on(u):
        chunk, low, count = place(u)
        j = chunk - 2 * (1 - y)
        core_copy(u).wait_recv()

        @pl.loop(low // 2, (low + count) // 2)
        def _(x):
            for i in range(packs):
                summed[j, i, x] = image[chunk, packs * core + i, x] + from_core[chunk, i, x]

        out_copy(u).start()

    def finish(u, others):
        chunk, _, _ = place(u)
        j = chunk - 2 * y
        core_copy(u).wait_recv()
        for w in others:
            out_copy(w).wait_recv()

        @pl.loop(0, block // 2)
        def _(x):
            low = first_half[:depth_out]
            for i in range(packs):
                mine = image[chunk, packs * core + i, x] + from_core[chunk, i, x]
                theirs = from_pair[j, i, x]
                left = jnp.where(y == 0, mine, theirs) * scale
                right = jnp.where(y == 0, theirs, mine) * scale
                result[i, j * block + 2 * x] = jnp.where(low, left, pltpu.roll(right, lanes, 1))
                second = jnp.where(low, pltpu.roll(left, lanes, 1), right)
                result[i, j * block + 2 * x + 1] = second

        store_copy(j).start()

    loads[0].wait()
    loads[1].wait()
    send_halo(0)
    for load in loads[2:]:
        load.wait()
    mirror_steps(0, block - 1, block)
    part_steps(1, 0, 0)
    pack(0, 0)
    pair_copy(0, 0).start()
    start_away(0, 0, 0)
    start_near(0, 0, 0)
    mirror_steps(0, 1, block - 2)
    part_steps(1, 0, 1)
    pack(0, 1)
    wait_halo(0)
    both_sides(0, 0, 1)
    send_halo(1)
    pair_copy(0, 1).start()
    start_near(0, 1, 0)
    steps(2, 3, planes - 3)
    steps(3, 4, planes - 4)
    for i in range(3):
        pack(1, i)
    start_away(1, 0, 0)
    relay(0, 0)
    wait_halo(1)
    both_sides(1, 0, 2)
    send_halo(2)
    for i in (2, 3):
        pack(0, i)
        pair_copy(0, i).start()
        start_away(0, i, 0)
        start_near(0, i, 0)
    start_away(1, 1, 0)
    both_sides(2, 1, 3)
    relay(0, 1)
    wait_halo(2)
    both_sides(2, 0, 1)
    send_halo(3)
    for i in (2, 0, 1):
        pair_copy(1, i).start()
    both_sides(3, 1, 4)
    relay(0, 2)
    relay(0, 3)
    for i in (2, 0, 1):
        start_near(1, i, 0)
    near, far = range(block + 1), range(2 * block + 1, HALF + 1)
    rest, most = range(block + 1, HALF + 1), range(2 * block + 1)
    middle = range(block + 1, 2 * block + 1)

    for load in matrices:
        load.wait()
    image_chunk(0, 1, near, True)
    image_chunk(0, 2, near, True)
    wait_halo(3)
    both_sides(3, 0, 1)
    for i in (3, 4):
        pack(1, i)
        pair_copy(1, i).start()
        start_away(1, i, 0)
        start_near(1, i, 0)
    for at in (-3, -2, -1, 4, 5, 6):
        wait_far(0, at)
    image_chunk(0, 1, rest)
    relay(1, 2)
    image_chunk(0, 2, rest)
    for i in range(2):
        pair_copy(1, i).wait_recv()
        start_away(1, i, 1)
    image_chunk(0, 0, range(HALF + 1), True)
    relay(1, 3)
    image_chunk(0, 3, range(HALF + 1), True)
    relay(1, 4)
    for i in (1, 0):
        start_near(1, i, 1)
    wait_far(1, 4)
    image_unit(1, 0, most)
    wait_far(1, 5)
    image_chunk(1, 3 - 3 * y, most)
    wait_far(1, -1)
    image_unit(1, 0, far)
    core_copy(0).start()
    image_unit(1, 3, most)
    pass_on(0)
    image_unit(1, 4, near)
    wait_far(1, 6, (4,))
    image_unit(1, 1, far)
    core_copy(1).start()
    wait_far(1, -2)
    wait_far(1, -3)
    image_unit(1, 3, far)
    core_copy(3).start()
    pass_on(1)
    image_unit(1, 4, middle)
    wait_far(1, 6, (0, 1))
    image_unit(1, 2, far)
    core_copy(2).start()
    image_unit(1, 4, far)
    core_copy(4).start()
    pass_on(2)
    finish(3, (0,))
    finish(4, (1, 2))
    for j in range(2):
        store_copy(j).wait()

    for t in range(STEPS):
        @pl.when(me < n - 1)
        def _():
            halo(t, 0).wait_send()

        @pl.when(me > 0)
        def _():
            halo(t, 1).wait_send()

    for g in range(IMAGES):
        for i in range(len(parts[g])):
            pair_copy(g, i).wait_send()
            for relayed in range(2):
                if relayed or inner(g, i):
                    @pl.when(has_away)
                    def _():
                        away_copy(g, i, relayed).wait_send()
                if not relayed or inner(g, i):
                    @pl.when(has_near)
                    def _():
                        near_copy(g, i, relayed).wait_send()

    for u in range(len(units)):
        core_copy(u).wait_send()
    for u in range(3):
        out_copy(u).wait_send()


def solution(mesh):
    n = mesh.shape["gx"]
    cores = mesh.shape["shot"]

    def local(src_now, src_prev, rec_now, rec_prev, courant_sq, wavelet, traces, positions):
        shots, planes, depth, width = src_now.shape
        depth_out = depth // 2
        reach = depth_out + (ANGLES - 1) * HALF // ANGLES
        rows = min(depth, -(-(reach + STEPS - 1) // 8) * 8)
        block = planes // 2
        assert n % 2 == 0 and cores == 2 and shots == 2 and 3 * block == HALF and block % 4 == 0 and width % 2 == 0
        angles_out = ANGLES // cores
        scale = 1.0 / math.sqrt(LAGS * shots * cores * IMAGES)
        smem = pl.BlockSpec(memory_space=pltpu.SMEM)
        hbm = pl.BlockSpec(memory_space=pl.ANY)
        matrices = [
            jnp.asarray(slant_matrix(group, depth_out, rows), jnp.bfloat16)
            for group in lag_groups(block)
        ]
        f32 = jnp.float32
        dma = pltpu.SemaphoreType.DMA
        return pl.pallas_call(
            functools.partial(kernel, n, scale, rows, reach),
            out_shape=jax.ShapeDtypeStruct((angles_out, planes, depth_out, width), f32),
            in_specs=[smem] * 3 + [hbm] * 8,
            out_specs=hbm,
            scratch_shapes=[
                pltpu.VMEM((STEPS + 2, 2, shots, planes + 2, depth, width), f32),
                pltpu.VMEM((planes, depth, width), f32),
                pltpu.VMEM((IMAGES, 2, 2 * planes + 2 * HALF, rows, width), f32),
                pltpu.VMEM((IMAGES, 2, planes, rows, width), f32),
                pltpu.VMEM((4, ANGLES, block // 2, depth_out, width), f32),
                pltpu.VMEM((4, angles_out, block // 2, depth_out, width), f32),
                pltpu.VMEM((2, angles_out, block // 2, depth_out, width), f32),
                pltpu.VMEM((2, angles_out, block // 2, depth_out, width), f32),
                *[pltpu.VMEM(m.shape, jnp.bfloat16) for m in matrices],
                *[pltpu.VMEM((m.shape[1], 2 * width), jnp.bfloat16) for m in matrices],
                pltpu.VMEM((angles_out, planes, depth_out, width), f32),
                dma((8,)),
                dma((2,)),
                dma((STEPS, 2)),
                dma((STEPS, 2)),
                dma((IMAGES, 5)),
                dma((IMAGES, 5)),
                dma((IMAGES, 5, 2)),
                dma((IMAGES, 5, 2)),
                dma((IMAGES, 5, 2)),
                dma((IMAGES, 5, 2)),
                dma((5,)),
                dma((5,)),
                dma((3,)),
                dma((3,)),
            ],
            compiler_params=pltpu.CompilerParams(
                collective_id=0, has_side_effects=True, vmem_limit_bytes=60 * 1024 * 1024
            ),
        )(positions, wavelet, traces, src_now, src_prev, rec_now, rec_prev, courant_sq, *matrices)

    placed = (
        P(("groups", "shot"), "gx", None, None),
        P(("groups", "shot"), "gx", None, None),
        P(("groups", "shot"), "gx", None, None),
        P(("groups", "shot"), "gx", None, None),
        P(("groups", "gx"), None, None),
        P(("groups", "shot"), None),
        P(("groups", "shot"), None, "gx"),
        P(("groups", "shot"), None),
    )
    return jax.shard_map(
        local,
        mesh=mesh,
        in_specs=placed,
        out_specs=P(("groups", "shot"), "gx", None, None),
        check_vma=False,
    )
```

```python
import functools
import math

import jax
import jax.numpy as jnp
import numpy as np
from jax import lax
from jax.experimental import pallas as pl
from jax.experimental.pallas import tpu as pltpu
from jax.sharding import PartitionSpec as P

STEPS = 4
IMAGES = 2
LAGS = 49
ANGLES = 8
HALF = (LAGS - 1) // 2
MESH = pl.DeviceIdType.MESH


def lag_groups(block):
    edges = (-1, block, 2 * block, HALF)
    return [range(low + 1, high + 1) for low, high in zip(edges, edges[1:])]


def lag_rows(h, last, depth_out, rows):
    def kept(h):
        return -(-(depth_out + (ANGLES - 1) * h // ANGLES) // 8) * 8

    pair = h + 1 if last[0] % 2 == h % 2 else h - 1
    if pair > last[-1]:
        return min(rows, -(-kept(h) // 16) * 16)
    if (kept(h) + kept(pair)) % 16:
        return max(kept(h), kept(pair))
    return kept(h)


def slant_matrix(group, depth_out, rows):
    talls = [lag_rows(h, group, depth_out, rows) for h in group]
    total = sum(talls)
    ones = np.zeros((ANGLES * depth_out, 2 * total), np.float32)
    at = 0
    z = np.arange(depth_out)
    for h, tall in zip(group, talls):
        for a in range(ANGLES):
            for part in range(2):
                ones[a * depth_out + z, part * total + at + z + a * h // ANGLES] = 1.0
        at += tall
    return ones


def kernel(
    n,
    scale,
    rows,
    sent,
    positions,
    wavelet,
    traces,
    src_now,
    src_prev,
    rec_now,
    rec_prev,
    courant_hbm,
    near_hbm,
    middle_hbm,
    far_hbm,
    out,
    level,
    courant,
    window,
    outgoing,
    image,
    from_core,
    summed,
    from_pair,
    near_ones,
    middle_ones,
    far_ones,
    near_stack,
    middle_stack,
    far_stack,
    result,
    load_sem,
    store_sem,
    halo_send,
    halo_recv,
    pair_send,
    pair_recv,
    away_send,
    away_recv,
    near_send,
    near_recv,
    core_send,
    core_recv,
    out_send,
    out_recv,
):
    planes, depth, width = courant.shape
    block = planes // 2
    shots = src_now.shape[0]
    depth_out = out.shape[2]
    packs = from_core.shape[1]
    lanes = width // 2
    me = lax.axis_index("gx")
    core = lax.axis_index("shot")
    y = lax.rem(me, 2)
    pair = me + 1 - 2 * y
    other = 1 - core
    has_below = me >= 2
    has_above = me < n - 2
    has_away = ((y == 0) & has_above) | ((y == 1) & has_below)
    has_near = ((y == 0) & has_below) | ((y == 1) & has_above)
    parts = [
        ((block, block - 2), (2, block - 2), (planes - 2, 2), (0, 2)),
        ((block, 2), (block + 2, 2), (4, block - 4), (0, 4), (planes - 4, 4)),
    ]

    loads = []
    for i, (ref, k, f) in enumerate(
        ((src_now, 1, 0), (rec_now, 1, 1), (src_prev, 0, 0), (rec_prev, 0, 1))
    ):
        loads.append(
            pltpu.make_async_copy(ref, level.at[k, f, :, pl.ds(1, planes)], load_sem.at[i])
        )
    loads.append(pltpu.make_async_copy(courant_hbm, courant, load_sem.at[4]))
    for load in loads:
        load.start()
    ones = (near_ones, middle_ones, far_ones)
    stacks = (near_stack, middle_stack, far_stack)
    matrices = [
        pltpu.make_async_copy(ref, ones[k], load_sem.at[5 + k])
        for k, ref in enumerate((near_hbm, middle_hbm, far_hbm))
    ]
    for load in matrices:
        load.start()

    barrier = pltpu.get_barrier_semaphore()
    for step in (-2, -1, 1, 2):
        there = me + step

        @pl.when((there >= 0) & (there < n))
        def _():
            pl.semaphore_signal(barrier, inc=1, device_id={"gx": there}, device_id_type=MESH)

    pl.semaphore_signal(barrier, inc=1, device_id={"shot": other}, device_id_type=MESH)

    edge = jnp.zeros((rows, width), jnp.float32)
    full = jnp.zeros((depth, width), jnp.float32)

    @pl.when(me == 0)
    def _():
        for k in range(1, STEPS + 1):
            for f in range(2):
                for s in range(shots):
                    level[k, f, s, 0] = full

    @pl.when(me == n - 1)
    def _():
        for k in range(1, STEPS + 1):
            for f in range(2):
                for s in range(shots):
                    level[k, f, s, planes + 1] = full

    @pl.when(jnp.logical_not(has_below))
    def _():
        @pl.loop(0, HALF)
        def _(q):
            for g in range(IMAGES):
                for f in range(2):
                    window[g, f, q] = edge

    @pl.when(jnp.logical_not(has_above))
    def _():
        @pl.loop(0, HALF)
        def _(q):
            for g in range(IMAGES):
                for f in range(2):
                    window[g, f, HALF + 2 * planes + q] = edge

    peers = jnp.minimum(me, 2) + jnp.minimum(n - 1 - me, 2) + 1
    pl.semaphore_wait(barrier, peers)

    def halo(t, side):
        height = min(depth, sent + STEPS - 1 - t)
        kept = pl.ds(0, height)
        source, target = (planes, 0) if side == 0 else (1, planes + 1)
        return pltpu.make_async_remote_copy(
            src_ref=level.at[1 + t, :, :, source, kept],
            dst_ref=level.at[1 + t, :, :, target, kept],
            send_sem=halo_send.at[t, side],
            recv_sem=halo_recv.at[t, side],
            device_id={"gx": me + 1 if side == 0 else me - 1},
            device_id_type=MESH,
        )

    def send_halo(t):
        @pl.when(me < n - 1)
        def _():
            halo(t, 0).start()

        @pl.when(me > 0)
        def _():
            halo(t, 1).start()

    def wait_halo(t):
        @pl.when(me > 0)
        def _():
            halo(t, 0).wait_recv()

        @pl.when(me < n - 1)
        def _():
            halo(t, 1).wait_recv()

    z_row = lax.broadcasted_iota(jnp.int32, (rows, width), 0)
    y_lane = lax.broadcasted_iota(jnp.int32, (rows, width), 1)
    first = me * planes

    def plane_step(t, x):
        speed = courant[x - 1, :rows]
        tall = depth if t == 0 else rows
        for s in range(shots):
            for f in range(2):
                now_tall = level[1 + t, f, s, x, :tall]
                now = now_tall[:rows]
                low = level[1 + t, f, s, x - 1, :rows]
                high = level[1 + t, f, s, x + 1, :rows]
                zeros = jnp.zeros((1, width), jnp.float32)
                deeper = jnp.concatenate([now_tall[1:], zeros], axis=0)[:rows]
                shallower = jnp.concatenate([zeros, now[: rows - 1]], axis=0)
                left = jnp.where(y_lane == 0, 0.0, pltpu.roll(now, 1, 1))
                right = jnp.where(y_lane == width - 1, 0.0, pltpu.roll(now, width - 1, 1))
                beside = low + high + deeper + shallower + left + right
                nxt = 2.0 * now - level[t, f, s, x, :rows] + speed * (beside - 6.0 * now)
                if f == 0:
                    amount = jnp.where(first + x - 1 == positions[s, 0], wavelet[s, t], 0.0)
                    hit = (z_row == positions[s, 2]) & (y_lane == positions[s, 1])
                else:
                    amount = traces[s, STEPS - 1 - t, x - 1]
                    hit = (z_row == 0) & (y_lane == positions[s, 3])
                level[2 + t, f, s, x, :rows] = nxt + jnp.where(hit, amount, 0.0)

    def steps(t, low, high):
        @pl.loop(low + 1, high + 1)
        def _(x):
            plane_step(t, x)

    def both_sides(t, low, high):
        count = high - low

        @pl.loop(0, 2 * count)
        def _(i):
            side = i // count
            x = low + i - side * count
            plane_step(t, 1 + x + side * (planes - 1 - 2 * x))

    def begin(g, i, yy):
        low, count = parts[g][i]
        return low + yy * (planes - 2 * low - count)

    def mirror_steps(t, low, count):
        at = low + y * (planes - 2 * low - count)

        @pl.loop(0, count)
        def _(j):
            plane_step(t, 1 + at + j)

    def part_steps(t, g, i):
        at = begin(g, i, y)

        @pl.loop(0, parts[g][i][1])
        def _(j):
            plane_step(t, 1 + at + j)

    def pair_copy(g, i):
        at = begin(g, i, y)
        count = parts[g][i][1]
        return pltpu.make_async_remote_copy(
            src_ref=outgoing.at[g, :, pl.ds(at, count), pl.ds(0, sent)],
            dst_ref=window.at[g, :, pl.ds(HALF + planes * y + at, count), pl.ds(0, sent)],
            send_sem=pair_send.at[g, i],
            recv_sem=pair_recv.at[g, i],
            device_id={"gx": pair},
            device_id_type=MESH,
        )

    up_from, down_to = -block, HALF + 2 * planes

    def away_copy(g, i, relayed):
        yy = 1 - y if relayed else y
        at = planes * yy + begin(g, i, yy)
        count = parts[g][i][1]
        return pltpu.make_async_remote_copy(
            src_ref=window.at[g, :, pl.ds(HALF + at, count), pl.ds(0, sent)],
            dst_ref=window.at[
                g, :, pl.ds(at + up_from + y * (down_to - up_from), count), pl.ds(0, sent)
            ],
            send_sem=away_send.at[g, i, relayed],
            recv_sem=away_recv.at[g, i, relayed],
            device_id={"gx": me + 2 - 4 * y},
            device_id_type=MESH,
        )

    def near_copy(g, i, relayed):
        yy = 1 - y if relayed else y
        at = planes * yy + begin(g, i, yy)
        count = parts[g][i][1]
        return pltpu.make_async_remote_copy(
            src_ref=window.at[g, :, pl.ds(HALF + at, count), pl.ds(0, sent)],
            dst_ref=window.at[
                g, :, pl.ds(at + down_to + y * (up_from - down_to), count), pl.ds(0, sent)
            ],
            send_sem=near_send.at[g, i, relayed],
            recv_sem=near_recv.at[g, i, relayed],
            device_id={"gx": me - 2 + 4 * y},
            device_id_type=MESH,
        )

    def inner(g, i):
        return parts[g][i][0] >= block

    def start_away(g, i, relayed):
        if relayed or inner(g, i):
            @pl.when(has_away)
            def _():
                away_copy(g, i, relayed).start()

    def start_near(g, i, relayed):
        if not relayed or inner(g, i):
            @pl.when(has_near)
            def _():
                near_copy(g, i, relayed).start()

    first_half = y_lane < lanes

    def pack(g, i):
        at = begin(g, i, y)

        @pl.loop(0, parts[g][i][1])
        def _(j):
            x = at + j
            for f in range(2):
                one = level[2 * g + 3, f, 0, 1 + x, :rows]
                two = level[2 * g + 3, f, 1, 1 + x, :rows]
                halves = (
                    jnp.where(first_half, one, pltpu.roll(two, lanes, 1)),
                    jnp.where(first_half, pltpu.roll(one, lanes, 1), two),
                )
                window[g, f, HALF + planes * y + x] = jnp.where(y == 0, halves[0], halves[1])
                outgoing[g, f, x] = jnp.where(y == 0, halves[1], halves[0])

    def relay(g, i):
        pair_copy(g, i).wait_recv()
        start_away(g, i, 1)
        start_near(g, i, 1)

    def wait_far(g, block_at, only=None):
        if block_at < 0:
            relayed, low = ((1, 0), (1, block), (0, block))[-1 - block_at]
        else:
            relayed, low = ((0, 0), (0, block), (1, block))[block_at - 4]
        for i, (start, count) in enumerate(parts[g]):
            if low <= start < low + block and (only is None or i in only):
                @pl.when(has_near if block_at < 0 else has_away)
                def _():
                    (away_copy if block_at < 0 else near_copy)(g, i, relayed).wait_recv()

    units = ((2, 0, block), (3, 0, block // 2), (3, block // 2, block - block // 2), (1, 0, block), (0, 0, block))

    def place(u):
        m, low, count = units[u]
        return m + y * (3 - 2 * m), low + y * (block - 2 * low - count), count

    def image_unit(g, u, lags, fresh=False):
        chunk, low, count = place(u)
        image_chunk(g, chunk, lags, fresh, low, count)

    groups = lag_groups(block)
    low_half = lax.broadcasted_iota(jnp.int32, (8, width), 1) < lanes
    low_rows = [
        jnp.concatenate([low_half] * (tall // 8), axis=0) for tall in range(8, rows + 8, 8)
    ]
    known = lax.broadcasted_iota(jnp.int32, (8, width), 0) < sent - (rows - 8)

    def summed_product(g, at, h, tall):
        def one(at):
            value = window[g, 0, at - h, :tall] * window[g, 1, at + h, :tall]
            if h:
                value = value + window[g, 0, at + h, :tall] * window[g, 1, at - h, :tall]
            return value

        low = low_rows[tall // 8 - 1]
        even, odd = one(at), one(at + 1)
        folded = jnp.where(low, even, odd) + pltpu.roll(jnp.where(low, odd, even), lanes, 1)
        if tall == rows:
            last = jnp.where(known, folded[rows - 8 :], 0.0)
            folded = jnp.concatenate([folded[: rows - 8], last], axis=0)
        return folded

    def image_chunk(g, chunk, lags, fresh=False, low=0, count=block):
        used = [k for k in range(3) if groups[k][0] in lags]

        @pl.loop(0, count // 4)
        def _(q):
            x = low + 4 * q
            total = None
            for k in used:
                half_rows = stacks[k].shape[0] // 2
                group = groups[k]
                for j in range(2):
                    at = HALF + chunk * block + x + 2 * j
                    columns = slice(j * width, (j + 1) * width)
                    top = 0
                    for i in range(0, len(group), 2):
                        both = [
                            summed_product(g, at, h, lag_rows(h, group, depth_out, rows))
                            for h in group[i : i + 2]
                        ]
                        value = jnp.concatenate(both, axis=0) if len(both) > 1 else both[0]
                        high = value.astype(jnp.bfloat16)
                        rest_of = (value - high.astype(jnp.float32)).astype(jnp.bfloat16)
                        tall = value.shape[0]
                        stacks[k][top : top + tall, columns] = high
                        stacks[k][half_rows + top : half_rows + top + tall, columns] = rest_of
                        top += tall
                part = jnp.dot(ones[k][...], stacks[k][...], preferred_element_type=jnp.float32)
                total = part if total is None else total + part
            for j in range(2):
                for a in range(ANGLES):
                    piece = total[a * depth_out : (a + 1) * depth_out, j * width : (j + 1) * width]
                    if not fresh:
                        piece = piece + image[chunk, a, x // 2 + j]
                    image[chunk, a, x // 2 + j] = piece

    def core_copy(u):
        chunk, low, count = place(u)
        return pltpu.make_async_remote_copy(
            src_ref=image.at[chunk, pl.ds(packs * other, packs), pl.ds(low // 2, count // 2)],
            dst_ref=from_core.at[chunk, :, pl.ds(low // 2, count // 2)],
            send_sem=core_send.at[u],
            recv_sem=core_recv.at[u],
            device_id={"shot": other},
            device_id_type=MESH,
        )

    def out_copy(u):
        chunk, low, count = place(u)
        j = chunk - 2 * (1 - y)
        return pltpu.make_async_remote_copy(
            src_ref=summed.at[j, :, pl.ds(low // 2, count // 2)],
            dst_ref=from_pair.at[j, :, pl.ds(low // 2, count // 2)],
            send_sem=out_send.at[u],
            recv_sem=out_recv.at[u],
            device_id={"gx": pair},
            device_id_type=MESH,
        )

    def store_copy(j):
        kept = pl.ds(block * j, block)
        return pltpu.make_async_copy(result.at[:, kept], out.at[:, kept], store_sem.at[j])

    def pass_on(u):
        chunk, low, count = place(u)
        j = chunk - 2 * (1 - y)
        core_copy(u).wait_recv()

        @pl.loop(low // 2, (low + count) // 2)
        def _(x):
            for i in range(packs):
                summed[j, i, x] = image[chunk, packs * core + i, x] + from_core[chunk, i, x]

        out_copy(u).start()

    def finish(u, others):
        chunk, _, _ = place(u)
        j = chunk - 2 * y
        core_copy(u).wait_recv()
        for w in others:
            out_copy(w).wait_recv()

        @pl.loop(0, block // 2)
        def _(x):
            low = first_half[:depth_out]
            for i in range(packs):
                mine = image[chunk, packs * core + i, x] + from_core[chunk, i, x]
                theirs = from_pair[j, i, x]
                left = jnp.where(y == 0, mine, theirs) * scale
                right = jnp.where(y == 0, theirs, mine) * scale
                result[i, j * block + 2 * x] = jnp.where(low, left, pltpu.roll(right, lanes, 1))
                second = jnp.where(low, pltpu.roll(left, lanes, 1), right)
                result[i, j * block + 2 * x + 1] = second

        store_copy(j).start()

    loads[0].wait()
    loads[1].wait()
    send_halo(0)
    for load in loads[2:]:
        load.wait()
    mirror_steps(0, block - 1, block)
    part_steps(1, 0, 0)
    pack(0, 0)
    pair_copy(0, 0).start()
    start_away(0, 0, 0)
    start_near(0, 0, 0)
    mirror_steps(0, 1, block - 2)
    part_steps(1, 0, 1)
    pack(0, 1)
    wait_halo(0)
    both_sides(0, 0, 1)
    send_halo(1)
    pair_copy(0, 1).start()
    start_near(0, 1, 0)
    steps(2, 3, planes - 3)
    steps(3, 4, planes - 4)
    for i in range(3):
        pack(1, i)
    start_away(1, 0, 0)
    relay(0, 0)
    wait_halo(1)
    both_sides(1, 0, 2)
    send_halo(2)
    for i in (2, 3):
        pack(0, i)
        pair_copy(0, i).start()
        start_away(0, i, 0)
        start_near(0, i, 0)
    start_away(1, 1, 0)
    both_sides(2, 1, 3)
    relay(0, 1)
    wait_halo(2)
    both_sides(2, 0, 1)
    send_halo(3)
    for i in (2, 0, 1):
        pair_copy(1, i).start()
    both_sides(3, 1, 4)
    relay(0, 2)
    relay(0, 3)
    for i in (2, 0, 1):
        start_near(1, i, 0)
    near, far = range(block + 1), range(2 * block + 1, HALF + 1)
    rest, most = range(block + 1, HALF + 1), range(2 * block + 1)
    middle = range(block + 1, 2 * block + 1)

    for load in matrices:
        load.wait()
    image_chunk(0, 1, near, True)
    image_chunk(0, 2, near, True)
    wait_halo(3)
    both_sides(3, 0, 1)
    for i in (3, 4):
        pack(1, i)
        pair_copy(1, i).start()
        start_away(1, i, 0)
        start_near(1, i, 0)
    for at in (-3, -2, -1, 4, 5, 6):
        wait_far(0, at)
    image_chunk(0, 1, rest)
    relay(1, 2)
    image_chunk(0, 2, rest)
    for i in range(2):
        pair_copy(1, i).wait_recv()
        start_away(1, i, 1)
    image_chunk(0, 0, range(HALF + 1), True)
    relay(1, 3)
    image_chunk(0, 3, range(HALF + 1), True)
    relay(1, 4)
    for i in (1, 0):
        start_near(1, i, 1)
    wait_far(1, 4)
    image_unit(1, 0, most)
    wait_far(1, 5)
    image_chunk(1, 3 - 3 * y, most)
    wait_far(1, -1)
    image_unit(1, 0, far)
    core_copy(0).start()
    pass_on(0)
    image_unit(1, 3, most)
    image_unit(1, 4, near)
    wait_far(1, 6, (4,))
    image_unit(1, 1, far)
    core_copy(1).start()
    wait_far(1, -2)
    wait_far(1, -3)
    image_unit(1, 3, far)
    core_copy(3).start()
    pass_on(1)
    image_unit(1, 4, middle)
    wait_far(1, 6, (0, 1))
    image_unit(1, 2, far)
    core_copy(2).start()
    image_unit(1, 4, far)
    core_copy(4).start()
    pass_on(2)
    finish(3, (0,))
    finish(4, (1, 2))
    for j in range(2):
        store_copy(j).wait()

    for t in range(STEPS):
        @pl.when(me < n - 1)
        def _():
            halo(t, 0).wait_send()

        @pl.when(me > 0)
        def _():
            halo(t, 1).wait_send()

    for g in range(IMAGES):
        for i in range(len(parts[g])):
            pair_copy(g, i).wait_send()
            for relayed in range(2):
                if relayed or inner(g, i):
                    @pl.when(has_away)
                    def _():
                        away_copy(g, i, relayed).wait_send()
                if not relayed or inner(g, i):
                    @pl.when(has_near)
                    def _():
                        near_copy(g, i, relayed).wait_send()

    for u in range(len(units)):
        core_copy(u).wait_send()
    for u in range(3):
        out_copy(u).wait_send()


def solution(mesh):
    n = mesh.shape["gx"]
    cores = mesh.shape["shot"]

    def local(src_now, src_prev, rec_now, rec_prev, courant_sq, wavelet, traces, positions):
        shots, planes, depth, width = src_now.shape
        depth_out = depth // 2
        reach = depth_out + (ANGLES - 1) * HALF // ANGLES
        rows = min(depth, -(-(reach + STEPS - 1) // 8) * 8)
        block = planes // 2
        assert n % 2 == 0 and cores == 2 and shots == 2 and 3 * block == HALF and block % 4 == 0 and width % 2 == 0
        angles_out = ANGLES // cores
        scale = 1.0 / math.sqrt(LAGS * shots * cores * IMAGES)
        smem = pl.BlockSpec(memory_space=pltpu.SMEM)
        hbm = pl.BlockSpec(memory_space=pl.ANY)
        matrices = [
            jnp.asarray(slant_matrix(group, depth_out, rows), jnp.bfloat16)
            for group in lag_groups(block)
        ]
        f32 = jnp.float32
        dma = pltpu.SemaphoreType.DMA
        return pl.pallas_call(
            functools.partial(kernel, n, scale, rows, reach),
            out_shape=jax.ShapeDtypeStruct((angles_out, planes, depth_out, width), f32),
            in_specs=[smem] * 3 + [hbm] * 8,
            out_specs=hbm,
            scratch_shapes=[
                pltpu.VMEM((STEPS + 2, 2, shots, planes + 2, depth, width), f32),
                pltpu.VMEM((planes, depth, width), f32),
                pltpu.VMEM((IMAGES, 2, 2 * planes + 2 * HALF, rows, width), f32),
                pltpu.VMEM((IMAGES, 2, planes, rows, width), f32),
                pltpu.VMEM((4, ANGLES, block // 2, depth_out, width), f32),
                pltpu.VMEM((4, angles_out, block // 2, depth_out, width), f32),
                pltpu.VMEM((2, angles_out, block // 2, depth_out, width), f32),
                pltpu.VMEM((2, angles_out, block // 2, depth_out, width), f32),
                *[pltpu.VMEM(m.shape, jnp.bfloat16) for m in matrices],
                *[pltpu.VMEM((m.shape[1], 2 * width), jnp.bfloat16) for m in matrices],
                pltpu.VMEM((angles_out, planes, depth_out, width), f32),
                dma((8,)),
                dma((2,)),
                dma((STEPS, 2)),
                dma((STEPS, 2)),
                dma((IMAGES, 5)),
                dma((IMAGES, 5)),
                dma((IMAGES, 5, 2)),
                dma((IMAGES, 5, 2)),
                dma((IMAGES, 5, 2)),
                dma((IMAGES, 5, 2)),
                dma((5,)),
                dma((5,)),
                dma((3,)),
                dma((3,)),
            ],
            compiler_params=pltpu.CompilerParams(
                collective_id=0, has_side_effects=True, vmem_limit_bytes=60 * 1024 * 1024
            ),
        )(positions, wavelet, traces, src_now, src_prev, rec_now, rec_prev, courant_sq, *matrices)

    placed = (
        P(("groups", "shot"), "gx", None, None),
        P(("groups", "shot"), "gx", None, None),
        P(("groups", "shot"), "gx", None, None),
        P(("groups", "shot"), "gx", None, None),
        P(("groups", "gx"), None, None),
        P(("groups", "shot"), None),
        P(("groups", "shot"), None, "gx"),
        P(("groups", "shot"), None),
    )
    return jax.shard_map(
        local,
        mesh=mesh,
        in_specs=placed,
        out_specs=P(("groups", "shot"), "gx", None, None),
        check_vma=False,
    )
```
